512 devices in a mesh: dp: 32 (over x_lo, y, core), head: 16 (over z, x_hi).
Axes of the slice: x: 4 (x_hi: 2, x_lo: 2; x = x_hi * 2 + x_lo), y: 8, z: 8, core: 2. Of those that a mesh axis runs over, the one named last changes fastest.
Arguments:
- hidden_in: bfloat16 [8192, 7168], P('dp', 'head'), may hold values from -6 to 6
- latent_unnormed: bfloat16 [8192, 512], P('dp'), may hold values from -6 to 6
- unrotated_key: bfloat16 [8192, 64], P('dp'), may hold values from -6 to 6
- latent_norm_scale: float32 [512], replicated, may hold values from 0.1 to 1.9
- plain_query_rows: bfloat16 [8192, 16384], P('dp', 'head'), may hold values from -6 to 6
- rotated_query_rows: bfloat16 [8192, 8192], P('dp', 'head'), may hold values from -240 to 240
- key_up_matrix: bfloat16 [512, 16384], P('dp', 'head'), may hold values from -0.25 to 0.25
- value_up_matrix: bfloat16 [512, 16384], P('dp', 'head'), may hold values from -0.25 to 0.25
- output_cotangent: bfloat16 [8192, 16384], P('dp', 'head'), may hold values from -6 to 6
- down_weight: float32 [576, 7168], P('dp', 'head'), may hold values from -0.0625 to 0.0625
- first_moment: float32 [576, 7168], P('dp', 'head'), may hold values from -0.078125 to 0.078125
- second_moment: float32 [576, 7168], P('dp', 'head'), may hold values from 4e-08 to 4e-07
Outputs:
- query_grad_nope: bfloat16 [8192, 16384], P('dp', 'head')
- query_grad_rope: bfloat16 [8192, 8192], P('dp', 'head')
- new_weight: float32 [576, 7168], P('dp', 'head')
- new_first: float32 [576, 7168], P('dp', 'head')
- new_second: float32 [576, 7168], P('dp', 'head')
The draws below stay inside these ranges and needn't reach their ends.
All inputs are finite; a program needn't handle non-finite values.
Results may differ from the reference program's by a relative error of at most 0.011.
The reference program's roundings to bfloat16 on the way count: a program that leaves them out, or rounds other values in their place, can miss the bound.
Values may be sent and summed in bfloat16 or wider, within the bound.
A program may use at most 64 MiB of HBM per device.

```python
import math
import jax
import jax.numpy as jnp
from jax import lax

D = 7168
LATENT_RANK = 512
ROTARY_WIDTH = 64
PLAIN_WIDTH = 128
VALUE_WIDTH = 128
SEQUENCE_LENGTH = 256
HEAD_TOTAL = 128
KVO = 576
SEQUENCE_TOTAL = 32
TOKEN_TOTAL = 8192


def rope_pair(key):
    key_base = jax.random.fold_in(key, 101)
    query_base = jax.random.fold_in(key, 202)
    key_raw = jnp.clip(jax.random.normal(key_base, (TOKEN_TOTAL, ROTARY_WIDTH), jnp.float32), -6.0, 6.0)
    query_raw = jnp.clip(jax.random.normal(query_base, (TOKEN_TOTAL, HEAD_TOTAL, ROTARY_WIDTH), jnp.float32), -6.0, 6.0)
    return (key_raw, query_raw.reshape(TOKEN_TOTAL, HEAD_TOTAL * ROTARY_WIDTH))


def draw_unrotated_key(key, part):
    return rope_pair(key)[0].astype(jnp.bfloat16)


def draw_rotated_query_rows(key, part):
    return rope_pair(key)[1].astype(jnp.bfloat16)


def levels(key, shape, shards, smallest, largest):
    factor_of, own = 1.0, jax.random.fold_in(key, 6)
    for dim, parts in shards:
        heights = jnp.exp(jax.random.uniform(jax.random.fold_in(own, dim), (parts,), jnp.float32, smallest / len(shards), largest / len(shards)))
        factor_of = factor_of * jnp.repeat(heights, shape[dim] // parts).reshape([-1 if axis == dim else 1 for axis in range(len(shape))])
    return factor_of


def noise(own_key, dims, width, most, split=(), kind=jnp.bfloat16):
    drawn = jax.random.normal(own_key, dims, jnp.float32) * width
    if len(split) > 0:
        drawn = levels(own_key, dims, split, -0.22, 0.18) * drawn
    return jnp.clip(drawn, min=-most, max=most).astype(kind)


def setup_inputs(seed: int = 0) -> dict:
    key_list = jax.random.split(jax.random.key(seed), 13)
    hidden_in = noise(key_list[0], (TOKEN_TOTAL, D), 1.0, 6.0, ((0, 32), (1, 16)))
    latent_unnormed = noise(key_list[1], (TOKEN_TOTAL, LATENT_RANK), 1.0, 6.0, ((0, 32),))
    unrotated_key = draw_unrotated_key(jax.random.fold_in(key_list[12], 71), 0)
    latent_norm_scale = jnp.clip(1.0 + 0.18 * jax.random.normal(key_list[3], (LATENT_RANK,), jnp.float32), 0.1, 1.9)
    plain_query_rows = noise(key_list[4], (TOKEN_TOTAL, HEAD_TOTAL * PLAIN_WIDTH), 1.0, 6.0, ((0, 32), (1, 16)))
    rotated_query_rows = draw_rotated_query_rows(jax.random.fold_in(key_list[12], 71), 0)
    key_up_matrix = noise(key_list[6], (LATENT_RANK, HEAD_TOTAL * PLAIN_WIDTH), LATENT_RANK ** -0.5, 0.25, ((0, 32), (1, 16)))
    value_up_matrix = noise(key_list[7], (LATENT_RANK, HEAD_TOTAL * VALUE_WIDTH), LATENT_RANK ** -0.5, 0.25, ((0, 32), (1, 16)))
    output_cotangent = noise(key_list[8], (TOKEN_TOTAL, HEAD_TOTAL * VALUE_WIDTH), 1.0, 6.0, ((0, 32), (1, 16)))
    down_weight = noise(key_list[9], (KVO, D), D ** -0.5, 0.0625, ((0, 32), (1, 16)), jnp.float32)
    first_moment = noise(key_list[10], (KVO, D), 0.005, 0.078125, ((0, 32), (1, 16)), jnp.float32)
    second_moment = jnp.clip(jnp.exp(math.log(4.0000000467443897e-07) - 2.3025851 * jax.random.uniform(key_list[11], (KVO, D), jnp.float32) ** levels(key_list[11], (KVO, D), ((0, 32), (1, 16)), -0.2, 0.2)), 3.999999975690116e-08, 4.0000000467443897e-07)
    return {"hidden_in": hidden_in, "latent_unnormed": latent_unnormed, "unrotated_key": unrotated_key, "latent_norm_scale": latent_norm_scale, "plain_query_rows": plain_query_rows, "rotated_query_rows": rotated_query_rows, "key_up_matrix": key_up_matrix, "value_up_matrix": value_up_matrix, "output_cotangent": output_cotangent, "down_weight": down_weight, "first_moment": first_moment, "second_moment": second_moment}


norm_eps = 1e-06
beta_one = 0.9
beta_two = 0.999
adam_eps = 1e-08
learn_rate = 0.01
decay_rate = 0.1
bias_one = 1.0 - 0.9 ** 2
bias_two = 1.0 - 0.999 ** 2

def angle_tables(positions, rope_width):
    half_width = rope_width // 2
    inverse_freq = jnp.exp(jnp.arange(half_width, dtype=jnp.float32) * (-2.0 * math.log(10000.0) / rope_width))
    angles = positions.astype(jnp.float32)[:, None] * inverse_freq[None, :]
    return (jnp.cos(angles), jnp.sin(angles))

def rotate_key(key_rows, cos_table, sin_table):
    raw_key = key_rows.astype(jnp.float32)
    half_width = raw_key.shape[1] // 2
    first_half = raw_key[:, :half_width]
    second_half = raw_key[:, half_width:]
    turned = jnp.concatenate((first_half * cos_table - second_half * sin_table, first_half * sin_table + second_half * cos_table), axis=1)
    return turned.astype(jnp.bfloat16)

def latent_back(latent_sum, rope_sum, latent_in, inverse_rms, latent_norm_scale, cos_table, sin_table):
    latent_width = latent_in.shape[1]
    scaled_grad = latent_norm_scale * latent_sum
    inner_sum = lax.optimization_barrier(jnp.sum(latent_in * scaled_grad, axis=1, keepdims=True))
    latent_grad = inverse_rms * scaled_grad - latent_in * (inverse_rms * inverse_rms * inverse_rms) * inner_sum / latent_width
    half_width = rope_sum.shape[1] // 2
    grad_first = rope_sum[:, :half_width]
    grad_second = rope_sum[:, half_width:]
    rope_grad = jnp.concatenate((grad_first * cos_table + grad_second * sin_table, grad_second * cos_table - grad_first * sin_table), axis=1)
    return jnp.concatenate((latent_grad, rope_grad), axis=1).astype(jnp.bfloat16)

def rounded(values):
    return lax.optimization_barrier(values.astype(jnp.bfloat16))

def reference(hidden_in, latent_unnormed, unrotated_key, latent_norm_scale, plain_query_rows, rotated_query_rows, key_up_matrix, value_up_matrix, output_cotangent, down_weight, first_moment, second_moment):
    scale_factor = 1.0 / math.sqrt(PLAIN_WIDTH + ROTARY_WIDTH)
    cos_table, sin_table = angle_tables(jnp.arange(SEQUENCE_LENGTH, dtype=jnp.int32), ROTARY_WIDTH)
    causal = jnp.arange(SEQUENCE_LENGTH)[:, None] >= jnp.arange(SEQUENCE_LENGTH)[None, :]

    def one_sequence(item):
        latent_seq, key_seq, nope_seq, rope_seq, grad_seq = item
        key_rot = lax.optimization_barrier(rotate_key(key_seq, cos_table, sin_table)).astype(jnp.float32)
        latent_in = latent_seq.astype(jnp.float32)
        inverse_rms = lax.rsqrt(lax.optimization_barrier(jnp.mean(latent_in * latent_in, axis=1, keepdims=True)) + norm_eps)
        latent = (latent_in * inverse_rms * latent_norm_scale).astype(jnp.bfloat16)
        key_nope = rounded(jnp.dot(latent, key_up_matrix, preferred_element_type=jnp.float32)).astype(jnp.float32).reshape(SEQUENCE_LENGTH, HEAD_TOTAL, PLAIN_WIDTH)
        value_rows = rounded(jnp.dot(latent, value_up_matrix, preferred_element_type=jnp.float32)).astype(jnp.float32).reshape(SEQUENCE_LENGTH, HEAD_TOTAL, VALUE_WIDTH)
        nope_rows = nope_seq.astype(jnp.float32)
        rope_rows = rope_seq.astype(jnp.float32)
        grad_rows = grad_seq.astype(jnp.float32)
        scores = (jnp.einsum('thd,shd->hts', nope_rows, key_nope) + jnp.einsum('thd,sd->hts', rope_rows, key_rot)) * scale_factor
        scores = jnp.where(causal[None], scores, -1e+30)
        maxima = lax.optimization_barrier(jnp.max(scores, axis=-1, keepdims=True))
        exponent = jnp.exp(scores - maxima)
        probabilities = exponent / lax.optimization_barrier(jnp.sum(exponent, axis=-1, keepdims=True))
        prob_low = rounded(probabilities).astype(jnp.float32)
        attended = jnp.einsum('hts,shd->thd', prob_low, value_rows)
        delta_sum = jnp.einsum('thd,thd->ht', grad_rows, attended)
        grad_probs = jnp.einsum('thd,shd->hts', grad_rows, value_rows)
        grad_scores = probabilities * (grad_probs - delta_sum[:, :, None]) * scale_factor
        score_low = rounded(grad_scores).astype(jnp.float32)
        grad_nope_q = jnp.einsum('hts,shd->thd', score_low, key_nope).astype(jnp.bfloat16)
        grad_rope_q = jnp.einsum('hts,sd->thd', score_low, key_rot).astype(jnp.bfloat16)
        grad_key = rounded(jnp.einsum('hts,thd->shd', score_low, nope_rows)).reshape(SEQUENCE_LENGTH, HEAD_TOTAL * PLAIN_WIDTH)
        grad_value = rounded(jnp.einsum('hts,thd->shd', prob_low, grad_rows)).reshape(SEQUENCE_LENGTH, HEAD_TOTAL * VALUE_WIDTH)
        rope_sum = jnp.einsum('hts,thd->sd', score_low, rope_rows)
        latent_sum = jnp.dot(grad_key, key_up_matrix.T, preferred_element_type=jnp.float32) + jnp.dot(grad_value, value_up_matrix.T, preferred_element_type=jnp.float32)
        kv_rows = latent_back(latent_sum, rope_sum, latent_in, inverse_rms, latent_norm_scale, cos_table, sin_table)
        return (grad_nope_q.reshape(SEQUENCE_LENGTH, HEAD_TOTAL * PLAIN_WIDTH), grad_rope_q.reshape(SEQUENCE_LENGTH, HEAD_TOTAL * ROTARY_WIDTH), kv_rows)
    entry_list = (latent_unnormed.reshape(SEQUENCE_TOTAL, SEQUENCE_LENGTH, LATENT_RANK), unrotated_key.reshape(SEQUENCE_TOTAL, SEQUENCE_LENGTH, ROTARY_WIDTH), plain_query_rows.reshape(SEQUENCE_TOTAL, SEQUENCE_LENGTH, HEAD_TOTAL, PLAIN_WIDTH), rotated_query_rows.reshape(SEQUENCE_TOTAL, SEQUENCE_LENGTH, HEAD_TOTAL, ROTARY_WIDTH), output_cotangent.reshape(SEQUENCE_TOTAL, SEQUENCE_LENGTH, HEAD_TOTAL, VALUE_WIDTH))
    grads_nope, grads_rope, kv_all = lax.map(one_sequence, entry_list)
    kv_grad = kv_all.reshape(TOKEN_TOTAL, KVO)
    weight_grad = jnp.dot(kv_grad.T, hidden_in, preferred_element_type=jnp.float32) / TOKEN_TOTAL
    new_first = beta_one * first_moment + (1.0 - beta_one) * weight_grad
    new_second = beta_two * second_moment + (1.0 - beta_two) * weight_grad * weight_grad
    direction = new_first / bias_one / (jnp.sqrt(new_second / bias_two) + adam_eps)
    new_weight = down_weight - learn_rate * (direction + decay_rate * down_weight)
    return (grads_nope.reshape(TOKEN_TOTAL, HEAD_TOTAL * PLAIN_WIDTH), grads_rope.reshape(TOKEN_TOTAL, HEAD_TOTAL * ROTARY_WIDTH), new_weight, new_first, new_second)
```

```python
import functools
import math

import jax
import jax.numpy as jnp
import numpy as np
from jax import lax
from jax.experimental import pallas as pl
from jax.experimental.pallas import tpu as pltpu
from jax.sharding import PartitionSpec as P

SEQUENCE_LENGTH = 256

norm_eps = 1e-06
beta_one = 0.9
beta_two = 0.999
adam_eps = 1e-08
learn_rate = 0.01
decay_rate = 0.1
bias_one = 1.0 - 0.9**2
bias_two = 1.0 - 0.999**2

MESH = pl.DeviceIdType.MESH
BF16 = jnp.bfloat16
F32 = jnp.float32

Y_SIZE = 8
CHIPS = 16
HEAD_RANKS = 16
LANES = 640
CHUNK = 16
SLOT = 32
VMEM_SPEC = pl.BlockSpec(memory_space=pltpu.VMEM)


def angle_tables(rope_width):
    half_width = rope_width // 2
    inverse_freq = np.exp(
        np.arange(half_width, dtype=np.float32)
        * np.float32(-2.0 * math.log(10000.0) / rope_width)
    ).astype(np.float32)
    angles = np.arange(SEQUENCE_LENGTH, dtype=np.float32)[:, None] * inverse_freq[None, :]
    return np.cos(angles).astype(np.float32), np.sin(angles).astype(np.float32)


def gather_kernel(
    key_ref, value_ref, key_out, value_out,
    y_send, y_recv, x_send, x_recv, c_send, c_recv, own_sem,
):
    dp = lax.axis_index("dp")
    core = lax.rem(dp, 2)
    chip = dp // 2
    y_pos = lax.rem(chip, Y_SIZE)
    x_pos = chip // Y_SIZE

    def place(x, y, c):
        return (x * Y_SIZE + lax.rem(y + Y_SIZE, Y_SIZE)) * 2 + c

    other_x = 1 - x_pos
    ups = (place(x_pos, y_pos + 1, core), place(x_pos, y_pos - 1, core))
    x_partner = place(other_x, y_pos, core)
    c_partner = place(x_pos, y_pos, 1 - core)

    barrier = pltpu.get_barrier_semaphore()
    for peer in (ups[0], ups[1], x_partner, c_partner):
        pl.semaphore_signal(barrier, inc=1, device_id={"dp": peer}, device_id_type=MESH)
    pl.semaphore_wait(barrier, 4)

    rows_in = key_ref.shape[0]
    sources = (key_ref, value_ref)
    outs = (key_out, value_out)

    def rows_of(index):
        return pl.ds(pl.multiple_of(index * rows_in, rows_in), rows_in)

    def send(w, src, block, sems, e, peer):
        copy = pltpu.make_async_remote_copy(
            src_ref=src,
            dst_ref=outs[w].at[rows_of(block)],
            send_sem=sems[0].at[e],
            recv_sem=sems[1].at[e],
            device_id={"dp": peer},
            device_id_type=MESH,
        )
        copy.start()
        return copy

    y_sems, x_sems, c_sems = (y_send, y_recv), (x_send, x_recv), (c_send, c_recv)
    steps = {(0, 0): 4, (0, 1): 3, (1, 0): 3, (1, 1): 4}
    event = {}
    for s in range(1, 5):
        for p in range(2):
            for w in range(2):
                for d in range(2):
                    if s <= steps[(w, d)]:
                        event[(s, p, w, d)] = len(event)
    y_copies, x_copies, c_copies = {}, {}, {}

    for w in range(2):
        x_copies[w] = send(w, sources[w], dp, x_sems, w, x_partner)
    for w in range(2):
        for d in range(2):
            e = event[(1, 0, w, d)]
            y_copies[e] = send(w, sources[w], dp, y_sems, e, ups[d])
    for w in range(2):
        c_copies[w] = send(w, sources[w], dp, c_sems, w, c_partner)
    own = []
    for w in range(2):
        copy = pltpu.make_async_copy(sources[w], outs[w].at[rows_of(dp)], own_sem.at[w])
        copy.start()
        own.append(copy)
    for w in range(2):
        x_copies[w].wait_recv()
        view = outs[w].at[rows_of(x_partner)]
        for d in range(2):
            e = event[(1, 1, w, d)]
            y_copies[e] = send(w, view, x_partner, y_sems, e, ups[d])
        c_copies[2 + w] = send(w, view, x_partner, c_sems, 2 + w, c_partner)
    for (s, p, w, d), e in event.items():
        x = x_pos if p == 0 else other_x
        block = place(x, y_pos - s if d == 0 else y_pos + s, core)
        y_copies[e].wait_recv()
        view = outs[w].at[rows_of(block)]
        if s < steps[(w, d)]:
            n = event[(s + 1, p, w, d)]
            y_copies[n] = send(w, view, block, y_sems, n, ups[d])
        c_copies[4 + e] = send(w, view, block, c_sems, 4 + e, c_partner)
    for copy in own:
        copy.wait()
    for copy in x_copies.values():
        copy.wait_send()
    for copy in y_copies.values():
        copy.wait_send()
    for copy in c_copies.values():
        copy.wait()


def gather_up(key_up, value_up, dp_size):
    rows, cols = key_up.shape
    full = jax.ShapeDtypeStruct((rows * dp_size, cols), key_up.dtype)
    dma = pltpu.SemaphoreType.DMA
    return pl.pallas_call(
        gather_kernel,
        out_shape=(full, full),
        in_specs=[VMEM_SPEC] * 2,
        out_specs=(VMEM_SPEC, VMEM_SPEC),
        scratch_shapes=[
            dma((28,)), dma((28,)), dma((2,)), dma((2,)), dma((32,)), dma((32,)), dma((2,)),
        ],
        compiler_params=pltpu.CompilerParams(collective_id=0, has_side_effects=True),
        name="gather_up",
    )(key_up, value_up)


def dot(a, b, dims):
    return lax.dot_general(a, b, (dims, ((), ())), preferred_element_type=F32)


NN = ((1,), (0,))
NT = ((1,), (1,))
TN = ((0,), (0,))


def attention_kernel(
    scale_factor,
    latent_ref, raw_ref, gain_ref, cos_ref, sin_ref,
    query_ref, rope_ref, cot_ref, key_up_ref, value_up_ref,
    grad_query_ref, grad_rope_ref, part_ref,
    latent, key_rot, total, rope_total,
):
    step = pl.program_id(0)
    rank = latent_ref.shape[1]
    rope_width = raw_ref.shape[1]
    half = rope_width // 2

    @pl.when(step == 0)
    def _():
        x = latent_ref[...].astype(F32)
        inv = lax.rsqrt(jnp.mean(x * x, axis=1, keepdims=True) + norm_eps)
        latent[...] = (x * inv * gain_ref[...]).astype(BF16)
        raw = raw_ref[...].astype(F32)
        u, w = raw[:, :half], raw[:, half:]
        cos, sin = cos_ref[...], sin_ref[...]
        key_rot[...] = jnp.concatenate((u * cos - w * sin, u * sin + w * cos), axis=1).astype(BF16)
        total[...] = jnp.zeros_like(total)
        rope_total[...] = jnp.zeros_like(rope_total)

    tokens = latent_ref.shape[0]
    width = query_ref.shape[1] // 2
    keys2 = dot(latent[...], key_up_ref[...], NN).astype(BF16)
    values2 = dot(latent[...], value_up_ref[...], NN).astype(BF16)
    rot = key_rot[...]
    causal = lax.broadcasted_iota(jnp.int32, (tokens, tokens), 0) >= lax.broadcasted_iota(
        jnp.int32, (tokens, tokens), 1
    )
    grad_keys, grad_values, grad_ropes = [], [], []
    for h in range(2):
        cols = slice(h * width, (h + 1) * width)
        query = query_ref[:, cols]
        rope = rope_ref[:, h * rope_width : (h + 1) * rope_width]
        cot = cot_ref[:, cols]
        key = keys2[:, cols]
        value = values2[:, cols]
        scores = (dot(query, key, NT) + dot(rope, rot, NT)) * scale_factor
        scores = jnp.where(causal, scores, -1e30)
        grown = jnp.exp(scores - jnp.max(scores, axis=1, keepdims=True))
        probs = grown / jnp.sum(grown, axis=1, keepdims=True)
        prob_low = probs.astype(BF16)
        grad_probs = dot(cot, value, NT)
        delta = jnp.sum(prob_low.astype(F32) * grad_probs, axis=1, keepdims=True)
        score_low = (probs * (grad_probs - delta) * scale_factor).astype(BF16)
        grad_query_ref[:, cols] = dot(score_low, key, NN).astype(BF16)
        grad_ropes.append(dot(score_low, rot, NN).astype(BF16))
        grad_keys.append(dot(score_low, query, TN).astype(BF16))
        grad_values.append(dot(prob_low, cot, TN).astype(BF16))
        rope_total[...] += dot(score_low, rope, TN)
    grad_rope_ref[...] = jnp.concatenate(grad_ropes, axis=1)
    total[...] += dot(jnp.concatenate(grad_keys, axis=1), key_up_ref[...], NT) + dot(
        jnp.concatenate(grad_values, axis=1), value_up_ref[...], NT
    )

    @pl.when(step == pl.num_programs(0) - 1)
    def _():
        part_ref[:, :rank] = total[...].astype(BF16)
        part_ref[:, rank:] = jnp.concatenate(
            (rope_total[...], jnp.zeros((tokens, LANES - rank - rope_width), F32)), axis=1
        ).astype(BF16)


def attention_back(latent_in, raw_key, gain, cos, sin, query, rope, cot, key_full, value_full):
    tokens, rank = latent_in.shape
    rope_width = raw_key.shape[1]
    heads = rope.shape[1] // rope_width
    width = query.shape[1] // heads
    whole = lambda a: pl.BlockSpec(a.shape, lambda i: (0, 0))
    cut = lambda rows, cols: pl.BlockSpec((rows, cols), lambda i: (0, i))
    scale_factor = 1.0 / math.sqrt(width + rope_width)
    return pl.pallas_call(
        functools.partial(attention_kernel, scale_factor),
        grid=(heads // 2,),
        out_shape=(
            jax.ShapeDtypeStruct(query.shape, BF16),
            jax.ShapeDtypeStruct(rope.shape, BF16),
            jax.ShapeDtypeStruct((tokens, LANES), BF16),
        ),
        in_specs=[
            whole(latent_in), whole(raw_key), whole(gain), whole(cos), whole(sin),
            cut(tokens, 2 * width), cut(tokens, 2 * rope_width), cut(tokens, 2 * width),
            cut(rank, 2 * width), cut(rank, 2 * width),
        ],
        out_specs=(
            cut(tokens, 2 * width),
            cut(tokens, 2 * rope_width),
            pl.BlockSpec((tokens, LANES), lambda i: (0, 0)),
        ),
        scratch_shapes=[
            pltpu.VMEM((tokens, rank), BF16),
            pltpu.VMEM((tokens, rope_width), BF16),
            pltpu.VMEM((tokens, rank), F32),
            pltpu.VMEM((tokens, rope_width), F32),
        ],
        name="attention_back",
    )(latent_in, raw_key, gain, cos, sin, query, rope, cot, key_full, value_full)


def tail_kernel(
    part_ref, latent_ref, gain_ref, cos_ref, sin_ref, hidden_ref, out_ref,
    sum_recv, kv_own, kv_all, wide, core_out, core_in, chip_out, chip_in,
    s1, r1, s2, r2, s3, r3, s4, r4,
):
    dp = lax.axis_index("dp")
    head = lax.axis_index("head")
    core = lax.rem(dp, 2)
    chip = dp // 2
    rank = latent_ref.shape[1]
    rope_width = 2 * cos_ref.shape[1]
    half = rope_width // 2
    rows_out = out_ref.shape[0]
    kv_width = rank + rope_width

    def head_peer(k):
        return lax.rem(head + k, HEAD_RANKS)

    def chip_peer(k):
        return lax.rem(chip + k, CHIPS)

    barrier = pltpu.get_barrier_semaphore()

    @pl.loop(1, HEAD_RANKS)
    def _(k):
        pl.semaphore_signal(barrier, inc=1, device_id={"head": head_peer(k)}, device_id_type=MESH)

    @pl.loop(1, CHIPS)
    def _(k):
        pl.semaphore_signal(
            barrier, inc=1, device_id={"dp": chip_peer(k) * 2 + core}, device_id_type=MESH
        )

    core_peer = chip * 2 + 1 - core
    pl.semaphore_signal(barrier, inc=1, device_id={"dp": core_peer}, device_id_type=MESH)
    pl.semaphore_wait(barrier, HEAD_RANKS - 1 + CHIPS - 1 + 1)

    def rows_of(index, size):
        return pl.ds(pl.multiple_of(index * size, size), size)

    def sum_copy(k):
        return pltpu.make_async_remote_copy(
            src_ref=part_ref.at[rows_of(head_peer(k), CHUNK)],
            dst_ref=sum_recv.at[k],
            send_sem=s1.at[k],
            recv_sem=r1.at[k],
            device_id={"head": head_peer(k)},
            device_id_type=MESH,
        )

    @pl.loop(1, HEAD_RANKS)
    def _(k):
        sum_copy(k).start()

    mine = rows_of(head, CHUNK)
    x = latent_ref[mine, :].astype(F32)
    inv = lax.rsqrt(jnp.mean(x * x, axis=1, keepdims=True) + norm_eps)
    cos, sin = cos_ref[mine, :], sin_ref[mine, :]
    total = part_ref[mine, :].astype(F32)

    @pl.loop(1, HEAD_RANKS)
    def _(k):
        sum_copy(k).wait()

    for k in range(1, HEAD_RANKS):
        total += sum_recv[k].astype(F32)
    scaled = gain_ref[...] * total[:, :rank]
    inner = jnp.sum(x * scaled, axis=1, keepdims=True)
    latent_grad = inv * scaled - x * (inv * inv * inv) * inner / rank
    g, q = total[:, rank : rank + half], total[:, rank + half : rank + rope_width]
    tail = jnp.concatenate(
        (
            g * cos + q * sin,
            q * cos - g * sin,
            jnp.zeros((CHUNK, LANES - kv_width), F32),
        ),
        axis=1,
    )
    kv_own[:, :rank] = latent_grad.astype(BF16)
    kv_own[:, rank:] = tail.astype(BF16)

    def kv_copy(k):
        return pltpu.make_async_remote_copy(
            src_ref=kv_own,
            dst_ref=kv_all.at[mine],
            send_sem=s2.at[k],
            recv_sem=r2.at[k],
            device_id={"head": head_peer(k)},
            device_id_type=MESH,
        )

    @pl.loop(1, HEAD_RANKS)
    def _(k):
        kv_copy(k).start()

    kv_all[mine, :] = kv_own[...]

    row = lax.broadcasted_iota(jnp.int32, (2 * CHIPS * SLOT, 1), 0)
    r = row % SLOT
    owner = row // SLOT
    source = ((owner % CHIPS) * 2 + owner // CHIPS) * rows_out + r
    source = jnp.where(r < rows_out, source, -1)
    column = lax.broadcasted_iota(jnp.int32, (2 * CHIPS * SLOT, LANES), 1)
    pick = jnp.where(column == source, 1.0, 0.0).astype(BF16)

    @pl.loop(1, HEAD_RANKS)
    def _(k):
        kv_copy(k).wait()

    picked = dot(pick, kv_all[...], NT).astype(BF16)
    wide[...] = dot(picked, hidden_ref[...], NN)

    span = CHIPS * SLOT
    core_out[...] = wide[rows_of(1 - core, span), :].astype(BF16)
    core_copy = pltpu.make_async_remote_copy(
        src_ref=core_out,
        dst_ref=core_in,
        send_sem=s3,
        recv_sem=r3,
        device_id={"dp": core_peer},
        device_id_type=MESH,
    )
    core_copy.start()
    core_copy.wait()
    chip_out[...] = (wide[rows_of(core, span), :] + core_in[...].astype(F32)).astype(BF16)

    def chip_copy(k):
        return pltpu.make_async_remote_copy(
            src_ref=chip_out.at[rows_of(chip_peer(k), SLOT)],
            dst_ref=chip_in.at[k],
            send_sem=s4.at[k],
            recv_sem=r4.at[k],
            device_id={"dp": chip_peer(k) * 2 + core},
            device_id_type=MESH,
        )

    @pl.loop(1, CHIPS)
    def _(k):
        chip_copy(k).start()

    own_rows = rows_of(chip, SLOT)
    first = wide[rows_of(core * CHIPS + chip, SLOT), :] + core_in[own_rows, :].astype(F32)

    @pl.loop(1, CHIPS)
    def _(k):
        chip_copy(k).wait()

    for k in range(1, CHIPS):
        first += chip_in[k].astype(F32)
    out_ref[...] = first[:rows_out, :]


def tail(part, latent_in, gain, cos, sin, hidden, rows_out):
    cols = hidden.shape[1]
    tokens = hidden.shape[0]
    dma = pltpu.SemaphoreType.DMA
    span = CHIPS * SLOT
    return pl.pallas_call(
        tail_kernel,
        out_shape=jax.ShapeDtypeStruct((rows_out, cols), F32),
        in_specs=[VMEM_SPEC] * 6,
        out_specs=VMEM_SPEC,
        scratch_shapes=[
            pltpu.VMEM((HEAD_RANKS, CHUNK, LANES), BF16),
            pltpu.VMEM((CHUNK, LANES), BF16),
            pltpu.VMEM((tokens, LANES), BF16),
            pltpu.VMEM((2 * span, cols), F32),
            pltpu.VMEM((span, cols), BF16),
            pltpu.VMEM((span, cols), BF16),
            pltpu.VMEM((span, cols), BF16),
            pltpu.VMEM((CHIPS, SLOT, cols), BF16),
            dma((HEAD_RANKS,)), dma((HEAD_RANKS,)), dma((HEAD_RANKS,)), dma((HEAD_RANKS,)),
            dma, dma, dma((CHIPS,)), dma((CHIPS,)),
        ],
        compiler_params=pltpu.CompilerParams(collective_id=1, has_side_effects=True),
        name="tail",
    )(part, latent_in, gain, cos, sin, hidden)


def local(
    hidden_in,
    latent_unnormed,
    unrotated_key,
    latent_norm_scale,
    plain_query_rows,
    rotated_query_rows,
    key_up_matrix,
    value_up_matrix,
    output_cotangent,
    down_weight,
    first_moment,
    second_moment,
):
    row_count = latent_unnormed.shape[0]
    dp_size = lax.axis_size("dp")
    cos, sin = angle_tables(unrotated_key.shape[1])
    cos, sin = jnp.asarray(cos), jnp.asarray(sin)
    gain = latent_norm_scale[None, :]
    key_full, value_full = gather_up(key_up_matrix, value_up_matrix, dp_size)
    grad_query, grad_rope, part = attention_back(
        latent_unnormed, unrotated_key, gain, cos, sin,
        plain_query_rows, rotated_query_rows, output_cotangent, key_full, value_full,
    )
    weight_sum = tail(
        part, latent_unnormed, gain, cos, sin, hidden_in, down_weight.shape[0]
    )
    weight_grad = weight_sum / (row_count * dp_size)
    new_first = beta_one * first_moment + (1.0 - beta_one) * weight_grad
    new_second = beta_two * second_moment + (1.0 - beta_two) * weight_grad * weight_grad
    direction = new_first / bias_one / (jnp.sqrt(new_second / bias_two) + adam_eps)
    new_weight = down_weight - learn_rate * (direction + decay_rate * down_weight)
    return grad_query, grad_rope, new_weight, new_first, new_second


def solution(mesh):
    placed = (
        P("dp", "head"),
        P("dp", None),
        P("dp", None),
        P(),
        P("dp", "head"),
        P("dp", "head"),
        P("dp", "head"),
        P("dp", "head"),
        P("dp", "head"),
        P("dp", "head"),
        P("dp", "head"),
        P("dp", "head"),
    )
    return jax.shard_map(
        local,
        mesh=mesh,
        in_specs=placed,
        out_specs=(
            P("dp", "head"),
            P("dp", "head"),
            P("dp", "head"),
            P("dp", "head"),
            P("dp", "head"),
        ),
        check_vma=False,
    )
```

```python
import functools
import math

import jax
import jax.numpy as jnp
import numpy as np
from jax import lax
from jax.experimental import pallas as pl
from jax.experimental.pallas import tpu as pltpu
from jax.sharding import PartitionSpec as P

SEQUENCE_LENGTH = 256

norm_eps = 1e-06
beta_one = 0.9
beta_two = 0.999
adam_eps = 1e-08
learn_rate = 0.01
decay_rate = 0.1
bias_one = 1.0 - 0.9**2
bias_two = 1.0 - 0.999**2

MESH = pl.DeviceIdType.MESH
BF16 = jnp.bfloat16
F32 = jnp.float32

Y_SIZE = 8
HEAD_RANKS = 16
LANES = 640
CHUNK = 16
SLOT = 24
QUAD = 4
VMEM_SPEC = pl.BlockSpec(memory_space=pltpu.VMEM)


def angle_tables(rope_width):
    half_width = rope_width // 2
    inverse_freq = np.exp(
        np.arange(half_width, dtype=np.float32)
        * np.float32(-2.0 * math.log(10000.0) / rope_width)
    ).astype(np.float32)
    angles = np.arange(SEQUENCE_LENGTH, dtype=np.float32)[:, None] * inverse_freq[None, :]
    return np.cos(angles).astype(np.float32), np.sin(angles).astype(np.float32)


def gather_kernel(
    key_ref, value_ref, hidden_ref, key_out, value_out, hidden_out,
    y_send, y_recv, x_send, x_recv, c_send, c_recv, own_sem, h_send, h_recv,
):
    dp = lax.axis_index("dp")
    core = lax.rem(dp, 2)
    chip = dp // 2
    y_pos = lax.rem(chip, Y_SIZE)
    x_pos = chip // Y_SIZE

    def place(x, y, c):
        return (x * Y_SIZE + lax.rem(y + Y_SIZE, Y_SIZE)) * 2 + c

    other_x = 1 - x_pos
    ups = (place(x_pos, y_pos + 1, core), place(x_pos, y_pos - 1, core))
    x_partner = place(other_x, y_pos, core)
    c_partner = place(x_pos, y_pos, 1 - core)

    barrier = pltpu.get_barrier_semaphore()
    for peer in (ups[0], ups[1], x_partner, c_partner):
        pl.semaphore_signal(barrier, inc=1, device_id={"dp": peer}, device_id_type=MESH)
    pl.semaphore_wait(barrier, 4)

    rows_in = key_ref.shape[0]
    sources = (key_ref, value_ref)
    outs = (key_out, value_out)

    def rows_of(index):
        return pl.ds(pl.multiple_of(index * rows_in, rows_in), rows_in)

    def send(w, src, block, sems, e, peer):
        copy = pltpu.make_async_remote_copy(
            src_ref=src,
            dst_ref=outs[w].at[rows_of(block)],
            send_sem=sems[0].at[e],
            recv_sem=sems[1].at[e],
            device_id={"dp": peer},
            device_id_type=MESH,
        )
        copy.start()
        return copy

    y_sems, x_sems, c_sems = (y_send, y_recv), (x_send, x_recv), (c_send, c_recv)
    steps = {(0, 0): 4, (0, 1): 3, (1, 0): 3, (1, 1): 4}
    event = {}
    for s in range(1, 5):
        for p in range(2):
            for w in range(2):
                for d in range(2):
                    if s <= steps[(w, d)]:
                        event[(s, p, w, d)] = len(event)
    y_copies, x_copies, c_copies = {}, {}, {}

    for w in range(2):
        x_copies[w] = send(w, sources[w], dp, x_sems, w, x_partner)
    for w in range(2):
        for d in range(2):
            e = event[(1, 0, w, d)]
            y_copies[e] = send(w, sources[w], dp, y_sems, e, ups[d])
    for w in range(2):
        c_copies[w] = send(w, sources[w], dp, c_sems, w, c_partner)
    own = []
    for w in range(2):
        copy = pltpu.make_async_copy(sources[w], outs[w].at[rows_of(dp)], own_sem.at[w])
        copy.start()
        own.append(copy)
    def hidden_rows(x, c):
        size = hidden_ref.shape[0]
        return hidden_out.at[pl.ds(pl.multiple_of((x * 2 + c) * size, size), size)]

    def send_hidden(src, dst, e, peer):
        copy = pltpu.make_async_remote_copy(
            src_ref=src,
            dst_ref=dst,
            send_sem=h_send.at[e],
            recv_sem=h_recv.at[e],
            device_id={"dp": peer},
            device_id_type=MESH,
        )
        copy.start()
        return copy

    hidden_x = send_hidden(hidden_ref, hidden_rows(x_pos, core), 0, x_partner)
    hidden_c = send_hidden(hidden_ref, hidden_rows(x_pos, core), 1, c_partner)
    copy = pltpu.make_async_copy(hidden_ref, hidden_rows(x_pos, core), own_sem.at[2])
    copy.start()
    own.append(copy)
    for w in range(2):
        x_copies[w].wait_recv()
        view = outs[w].at[rows_of(x_partner)]
        for d in range(2):
            e = event[(1, 1, w, d)]
            y_copies[e] = send(w, view, x_partner, y_sems, e, ups[d])
        c_copies[2 + w] = send(w, view, x_partner, c_sems, 2 + w, c_partner)
    for (s, p, w, d), e in event.items():
        x = x_pos if p == 0 else other_x
        block = place(x, y_pos - s if d == 0 else y_pos + s, core)
        y_copies[e].wait_recv()
        view = outs[w].at[rows_of(block)]
        if s < steps[(w, d)]:
            n = event[(s + 1, p, w, d)]
            y_copies[n] = send(w, view, block, y_sems, n, ups[d])
        c_copies[4 + e] = send(w, view, block, c_sems, 4 + e, c_partner)
    hidden_x.wait_recv()
    far = hidden_rows(other_x, core)
    hidden_d = send_hidden(far, far, 2, c_partner)
    for copy in own:
        copy.wait()
    for copy in x_copies.values():
        copy.wait_send()
    for copy in y_copies.values():
        copy.wait_send()
    for copy in c_copies.values():
        copy.wait()
    hidden_x.wait_send()
    hidden_c.wait()
    hidden_d.wait()


def gather_up(key_up, value_up, hidden, dp_size):
    rows, cols = key_up.shape
    full = jax.ShapeDtypeStruct((rows * dp_size, cols), key_up.dtype)
    dma = pltpu.SemaphoreType.DMA
    return pl.pallas_call(
        gather_kernel,
        out_shape=(
            full, full, jax.ShapeDtypeStruct((QUAD * hidden.shape[0], hidden.shape[1]), BF16)
        ),
        in_specs=[VMEM_SPEC] * 3,
        out_specs=(VMEM_SPEC,) * 3,
        scratch_shapes=[
            dma((28,)), dma((28,)), dma((2,)), dma((2,)), dma((32,)), dma((32,)), dma((3,)),
            dma((3,)), dma((3,)),
        ],
        compiler_params=pltpu.CompilerParams(collective_id=0, has_side_effects=True),
        name="gather_up",
    )(key_up, value_up, hidden)


def dot(a, b, dims):
    return lax.dot_general(a, b, (dims, ((), ())), preferred_element_type=F32)


NN = ((1,), (0,))
NT = ((1,), (1,))
TN = ((0,), (0,))


def attention_kernel(
    scale_factor,
    latent_ref, raw_ref, gain_ref, cos_ref, sin_ref,
    query_ref, rope_ref, cot_ref, key_up_ref, value_up_ref,
    grad_query_ref, grad_rope_ref, part_ref,
    latent, key_rot, total, rope_total,
):
    step = pl.program_id(0)
    rank = latent_ref.shape[1]
    rope_width = raw_ref.shape[1]
    half = rope_width // 2

    @pl.when(step == 0)
    def _():
        x = latent_ref[...].astype(F32)
        inv = lax.rsqrt(jnp.mean(x * x, axis=1, keepdims=True) + norm_eps)
        latent[...] = (x * inv * gain_ref[...]).astype(BF16)
        raw = raw_ref[...].astype(F32)
        u, w = raw[:, :half], raw[:, half:]
        cos, sin = cos_ref[...], sin_ref[...]
        key_rot[...] = jnp.concatenate((u * cos - w * sin, u * sin + w * cos), axis=1).astype(BF16)
        total[...] = jnp.zeros_like(total)
        rope_total[...] = jnp.zeros_like(rope_total)

    tokens = latent_ref.shape[0]
    width = query_ref.shape[1] // 2
    keys2 = dot(latent[...], key_up_ref[...], NN).astype(BF16)
    values2 = dot(latent[...], value_up_ref[...], NN).astype(BF16)
    rot = key_rot[...]
    causal = lax.broadcasted_iota(jnp.int32, (tokens, tokens), 0) >= lax.broadcasted_iota(
        jnp.int32, (tokens, tokens), 1
    )
    grad_keys, grad_values, grad_ropes = [], [], []
    for h in range(2):
        cols = slice(h * width, (h + 1) * width)
        query = query_ref[:, cols]
        rope = rope_ref[:, h * rope_width : (h + 1) * rope_width]
        cot = cot_ref[:, cols]
        key = keys2[:, cols]
        value = values2[:, cols]
        scores = (dot(query, key, NT) + dot(rope, rot, NT)) * scale_factor
        scores = jnp.where(causal, scores, -1e30)
        grown = jnp.exp(scores - jnp.max(scores, axis=1, keepdims=True))
        probs = grown / jnp.sum(grown, axis=1, keepdims=True)
        prob_low = probs.astype(BF16)
        grad_probs = dot(cot, value, NT)
        delta = jnp.sum(prob_low.astype(F32) * grad_probs, axis=1, keepdims=True)
        score_low = (probs * (grad_probs - delta) * scale_factor).astype(BF16)
        grad_query_ref[:, cols] = dot(score_low, key, NN).astype(BF16)
        grad_ropes.append(dot(score_low, rot, NN).astype(BF16))
        grad_keys.append(dot(score_low, query, TN).astype(BF16))
        grad_values.append(dot(prob_low, cot, TN).astype(BF16))
        rope_total[...] += dot(score_low, rope, TN)
    grad_rope_ref[...] = jnp.concatenate(grad_ropes, axis=1)
    total[...] += dot(jnp.concatenate(grad_keys, axis=1), key_up_ref[...], NT) + dot(
        jnp.concatenate(grad_values, axis=1), value_up_ref[...], NT
    )

    @pl.when(step == pl.num_programs(0) - 1)
    def _():
        part_ref[:, :rank] = total[...]
        part_ref[:, rank:] = jnp.concatenate(
            (rope_total[...], jnp.zeros((tokens, LANES - rank - rope_width), F32)), axis=1
        )


def attention_back(latent_in, raw_key, gain, cos, sin, query, rope, cot, key_full, value_full):
    tokens, rank = latent_in.shape
    rope_width = raw_key.shape[1]
    heads = rope.shape[1] // rope_width
    width = query.shape[1] // heads
    whole = lambda a: pl.BlockSpec(a.shape, lambda i: (0, 0))
    cut = lambda rows, cols: pl.BlockSpec((rows, cols), lambda i: (0, i))
    scale_factor = 1.0 / math.sqrt(width + rope_width)
    return pl.pallas_call(
        functools.partial(attention_kernel, scale_factor),
        grid=(heads // 2,),
        out_shape=(
            jax.ShapeDtypeStruct(query.shape, BF16),
            jax.ShapeDtypeStruct(rope.shape, BF16),
            jax.ShapeDtypeStruct((tokens, LANES), F32),
        ),
        in_specs=[
            whole(latent_in), whole(raw_key), whole(gain), whole(cos), whole(sin),
            cut(tokens, 2 * width), cut(tokens, 2 * rope_width), cut(tokens, 2 * width),
            cut(rank, 2 * width), cut(rank, 2 * width),
        ],
        out_specs=(
            cut(tokens, 2 * width),
            cut(tokens, 2 * rope_width),
            pl.BlockSpec((tokens, LANES), lambda i: (0, 0)),
        ),
        scratch_shapes=[
            pltpu.VMEM((tokens, rank), BF16),
            pltpu.VMEM((tokens, rope_width), BF16),
            pltpu.VMEM((tokens, rank), F32),
            pltpu.VMEM((tokens, rope_width), F32),
        ],
        name="attention_back",
    )(latent_in, raw_key, gain, cos, sin, query, rope, cot, key_full, value_full)


def tail_tables(rows_out):
    per_quad = Y_SIZE * rows_out

    def column(member, q):
        y, r = divmod(q, rows_out)
        return (((member // 2) * Y_SIZE + y) * 2 + member % 2) * rows_out + r

    extra = per_quad - 128
    order = np.full((1, (QUAD + 1) * 128), -1, np.int32)
    for member in range(QUAD):
        for q in range(per_quad):
            lane = member * 128 + q if q < 128 else QUAD * 128 + member * extra + q - 128
            order[0, lane] = column(member, q)
    rows = np.full((Y_SIZE * SLOT, 1), -1000, np.int32)
    for y in range(Y_SIZE):
        rows[y * SLOT : y * SLOT + rows_out, 0] = y * rows_out + np.arange(rows_out)
    return order, rows


def tail_kernel(
    part_ref, latent_ref, gain_ref, cos_ref, sin_ref, hidden_ref, order_ref, rows_ref, out_ref,
    sum_recv, kv_own, quad_out, quad_in, block_out, block_all, y_out, y_in,
    s1, r1, s2, r2, s3, r3, s4, r4,
):
    dp = lax.axis_index("dp")
    head = lax.axis_index("head")
    core = lax.rem(dp, 2)
    chip = dp // 2
    y_pos = lax.rem(chip, Y_SIZE)
    x_pos = chip // Y_SIZE
    member = x_pos * 2 + core
    rank = latent_ref.shape[1]
    tokens = latent_ref.shape[0]
    rope_width = 2 * cos_ref.shape[1]
    half = rope_width // 2
    rows_out = out_ref.shape[0]
    kv_width = rank + rope_width
    extra = Y_SIZE * rows_out - 128

    def head_peer(k):
        return lax.rem(head + k, HEAD_RANKS)

    def y_peer(k):
        return lax.rem(y_pos + k, Y_SIZE)

    def y_device(k):
        return (x_pos * Y_SIZE + y_peer(k)) * 2 + core

    def quad_peer(k):
        return lax.rem(member + k, QUAD)

    def quad_device(k):
        other = quad_peer(k)
        return ((other // 2) * Y_SIZE + y_pos) * 2 + lax.rem(other, 2)

    barrier = pltpu.get_barrier_semaphore()

    @pl.loop(1, HEAD_RANKS)
    def _(k):
        pl.semaphore_signal(barrier, inc=1, device_id={"head": head_peer(k)}, device_id_type=MESH)

    @pl.loop(1, Y_SIZE)
    def _(k):
        pl.semaphore_signal(barrier, inc=1, device_id={"dp": y_device(k)}, device_id_type=MESH)

    @pl.loop(1, QUAD)
    def _(k):
        pl.semaphore_signal(barrier, inc=1, device_id={"dp": quad_device(k)}, device_id_type=MESH)

    pl.semaphore_wait(barrier, HEAD_RANKS - 1 + Y_SIZE - 1 + QUAD - 1)

    def rows_of(index, size):
        return pl.ds(pl.multiple_of(index * size, size), size)

    def sum_copy(k):
        return pltpu.make_async_remote_copy(
            src_ref=part_ref.at[rows_of(head_peer(k), CHUNK)],
            dst_ref=sum_recv.at[k],
            send_sem=s1.at[k],
            recv_sem=r1.at[k],
            device_id={"head": head_peer(k)},
            device_id_type=MESH,
        )

    @pl.loop(1, HEAD_RANKS)
    def _(k):
        sum_copy(k).start()

    mine = rows_of(head, CHUNK)
    x = latent_ref[mine, :].astype(F32)
    inv = lax.rsqrt(jnp.mean(x * x, axis=1, keepdims=True) + norm_eps)
    cos, sin = cos_ref[mine, :], sin_ref[mine, :]
    total = part_ref[mine, :]
    iota = lax.broadcasted_iota(jnp.int32, (LANES, LANES), 0)
    select = jnp.where(iota == order_ref[...], 1.0, 0.0).astype(BF16)

    @pl.loop(1, HEAD_RANKS)
    def _(k):
        sum_copy(k).wait()

    for k in range(1, HEAD_RANKS):
        total += sum_recv[k]
    scaled = gain_ref[...] * total[:, :rank]
    inner = jnp.sum(x * scaled, axis=1, keepdims=True)
    latent_grad = inv * scaled - x * (inv * inv * inv) * inner / rank
    g, q = total[:, rank : rank + half], total[:, rank + half : rank + rope_width]
    rope_grad = jnp.concatenate(
        (
            g * cos + q * sin,
            q * cos - g * sin,
            jnp.zeros((CHUNK, LANES - kv_width), F32),
        ),
        axis=1,
    )
    kv_own[:, :rank] = latent_grad.astype(BF16)
    kv_own[:, rank:] = rope_grad.astype(BF16)

    sent = dot(kv_own[...], select, NN).astype(BF16)
    for m in range(QUAD):
        quad_out[m, 0] = sent[:, m * 128 : (m + 1) * 128]
        quad_out[m, 1] = sent[:, QUAD * 128 :]

    def quad_copy(k):
        return pltpu.make_async_remote_copy(
            src_ref=quad_out.at[quad_peer(k)],
            dst_ref=quad_in.at[member],
            send_sem=s2.at[k],
            recv_sem=r2.at[k],
            device_id={"dp": quad_device(k)},
            device_id_type=MESH,
        )

    for k in range(1, QUAD):
        quad_copy(k).start()
    quad_in[member] = quad_out[member]
    lane_in = lax.broadcasted_iota(jnp.int32, (128, 128), 0)
    lane_to = lax.broadcasted_iota(jnp.int32, (128, 128), 1)
    for k in range(1, QUAD):
        quad_copy(k).wait()
    rest = jnp.zeros((CHUNK, 128), F32)
    for m in range(QUAD):
        block_out[m] = quad_in[m, 0]
        inside = (lane_to >= m * extra) & (lane_to < (m + 1) * extra)
        move = inside & (lane_in - member * extra == lane_to - m * extra)
        rest += dot(quad_in[m, 1], jnp.where(move, 1.0, 0.0).astype(BF16), NN)
    block_out[QUAD] = rest.astype(BF16)

    def block_copy(k):
        return pltpu.make_async_remote_copy(
            src_ref=block_out,
            dst_ref=block_all.at[:, mine],
            send_sem=s3.at[k],
            recv_sem=r3.at[k],
            device_id={"head": head_peer(k)},
            device_id_type=MESH,
        )

    @pl.loop(1, HEAD_RANKS)
    def _(k):
        block_copy(k).start()

    block_all[:, mine, :] = block_out[...]
    q_row = rows_ref[...]
    lane = lax.broadcasted_iota(jnp.int32, (Y_SIZE * SLOT, 128), 1)
    pick = jnp.where(lane == q_row, 1.0, 0.0).astype(BF16)
    q_rest = jnp.where(q_row >= 128, q_row - 128, -1000)
    pick_rest = [
        jnp.where(lane == q_rest + m * extra, 1.0, 0.0).astype(BF16) for m in range(QUAD)
    ]

    @pl.loop(1, HEAD_RANKS)
    def _(k):
        block_copy(k).wait()

    grad = jnp.zeros((Y_SIZE * SLOT, hidden_ref.shape[1]), F32)
    for m in range(QUAD):
        picked = dot(pick, block_all[m], NT) + dot(pick_rest[m], block_all[QUAD], NT)
        grad += dot(
            picked.astype(BF16), hidden_ref[m * tokens : (m + 1) * tokens, :], NN
        )
    y_out[...] = grad

    def y_copy(k):
        return pltpu.make_async_remote_copy(
            src_ref=y_out.at[rows_of(y_peer(k), SLOT)],
            dst_ref=y_in.at[k],
            send_sem=s4.at[k],
            recv_sem=r4.at[k],
            device_id={"dp": y_device(k)},
            device_id_type=MESH,
        )

    @pl.loop(1, Y_SIZE)
    def _(k):
        y_copy(k).start()

    first = y_out[rows_of(y_pos, SLOT), :]

    @pl.loop(1, Y_SIZE)
    def _(k):
        y_copy(k).wait()

    for k in range(1, Y_SIZE):
        first += y_in[k]
    out_ref[...] = first[:rows_out, :]


def tail(part, latent_in, gain, cos, sin, hidden_quad, rows_out):
    tokens = latent_in.shape[0]
    cols = hidden_quad.shape[1]
    dma = pltpu.SemaphoreType.DMA
    order, rows = tail_tables(rows_out)
    return pl.pallas_call(
        tail_kernel,
        out_shape=jax.ShapeDtypeStruct((rows_out, cols), F32),
        in_specs=[VMEM_SPEC] * 8,
        out_specs=VMEM_SPEC,
        scratch_shapes=[
            pltpu.VMEM((HEAD_RANKS, CHUNK, LANES), F32),
            pltpu.VMEM((CHUNK, LANES), BF16),
            pltpu.VMEM((QUAD, 2, CHUNK, 128), BF16),
            pltpu.VMEM((QUAD, 2, CHUNK, 128), BF16),
            pltpu.VMEM((QUAD + 1, CHUNK, 128), BF16),
            pltpu.VMEM((QUAD + 1, tokens, 128), BF16),
            pltpu.VMEM((Y_SIZE * SLOT, cols), F32),
            pltpu.VMEM((Y_SIZE, SLOT, cols), F32),
            dma((HEAD_RANKS,)), dma((HEAD_RANKS,)), dma((QUAD,)), dma((QUAD,)),
            dma((HEAD_RANKS,)), dma((HEAD_RANKS,)), dma((Y_SIZE,)), dma((Y_SIZE,)),
        ],
        compiler_params=pltpu.CompilerParams(collective_id=1, has_side_effects=True),
        name="tail",
    )(part, latent_in, gain, cos, sin, hidden_quad, jnp.asarray(order), jnp.asarray(rows))


def local(
    hidden_in,
    latent_unnormed,
    unrotated_key,
    latent_norm_scale,
    plain_query_rows,
    rotated_query_rows,
    key_up_matrix,
    value_up_matrix,
    output_cotangent,
    down_weight,
    first_moment,
    second_moment,
):
    row_count = latent_unnormed.shape[0]
    dp_size = lax.axis_size("dp")
    cos, sin = angle_tables(unrotated_key.shape[1])
    cos, sin = jnp.asarray(cos), jnp.asarray(sin)
    gain = latent_norm_scale[None, :]
    key_full, value_full, hidden_quad = gather_up(
        key_up_matrix, value_up_matrix, hidden_in, dp_size
    )
    grad_query, grad_rope, part = attention_back(
        latent_unnormed, unrotated_key, gain, cos, sin,
        plain_query_rows, rotated_query_rows, output_cotangent, key_full, value_full,
    )
    weight_sum = tail(
        part, latent_unnormed, gain, cos, sin, hidden_quad, down_weight.shape[0]
    )
    weight_grad = weight_sum / (row_count * dp_size)
    new_first = beta_one * first_moment + (1.0 - beta_one) * weight_grad
    new_second = beta_two * second_moment + (1.0 - beta_two) * weight_grad * weight_grad
    direction = new_first / bias_one / (jnp.sqrt(new_second / bias_two) + adam_eps)
    new_weight = down_weight - learn_rate * (direction + decay_rate * down_weight)
    return grad_query, grad_rope, new_weight, new_first, new_second


def solution(mesh):
    placed = (
        P("dp", "head"),
        P("dp", None),
        P("dp", None),
        P(),
        P("dp", "head"),
        P("dp", "head"),
        P("dp", "head"),
        P("dp", "head"),
        P("dp", "head"),
        P("dp", "head"),
        P("dp", "head"),
        P("dp", "head"),
    )
    return jax.shard_map(
        local,
        mesh=mesh,
        in_specs=placed,
        out_specs=(
            P("dp", "head"),
            P("dp", "head"),
            P("dp", "head"),
            P("dp", "head"),
            P("dp", "head"),
        ),
        check_vma=False,
    )
```

```python
import functools
import math

import jax
import jax.numpy as jnp
import numpy as np
from jax import lax
from jax.experimental import pallas as pl
from jax.experimental.pallas import tpu as pltpu
from jax.sharding import PartitionSpec as P

SEQUENCE_LENGTH = 256

norm_eps = 1e-06
beta_one = 0.9
beta_two = 0.999
adam_eps = 1e-08
learn_rate = 0.01
decay_rate = 0.1
bias_one = 1.0 - 0.9**2
bias_two = 1.0 - 0.999**2

MESH = pl.DeviceIdType.MESH
BF16 = jnp.bfloat16
F32 = jnp.float32

Y_SIZE = 8
HEAD_RANKS = 16
LANES = 640
CHUNK = 16
SLOT = 24
PACKED = 64
QUAD = 4
VMEM_SPEC = pl.BlockSpec(memory_space=pltpu.VMEM)


def angle_tables(rope_width):
    half_width = rope_width // 2
    inverse_freq = np.exp(
        np.arange(half_width, dtype=np.float32)
        * np.float32(-2.0 * math.log(10000.0) / rope_width)
    ).astype(np.float32)
    angles = np.arange(SEQUENCE_LENGTH, dtype=np.float32)[:, None] * inverse_freq[None, :]
    return np.cos(angles).astype(np.float32), np.sin(angles).astype(np.float32)


def gather_kernel(
    key_ref, value_ref, hidden_ref, key_out, value_out, hidden_out,
    y_send, y_recv, x_send, x_recv, c_send, c_recv, own_sem, h_send, h_recv,
):
    dp = lax.axis_index("dp")
    core = lax.rem(dp, 2)
    chip = dp // 2
    y_pos = lax.rem(chip, Y_SIZE)
    x_pos = chip // Y_SIZE

    def place(x, y, c):
        return (x * Y_SIZE + lax.rem(y + Y_SIZE, Y_SIZE)) * 2 + c

    other_x = 1 - x_pos
    ups = (place(x_pos, y_pos + 1, core), place(x_pos, y_pos - 1, core))
    x_partner = place(other_x, y_pos, core)
    c_partner = place(x_pos, y_pos, 1 - core)

    barrier = pltpu.get_barrier_semaphore()
    for peer in (ups[0], ups[1], x_partner, c_partner):
        pl.semaphore_signal(barrier, inc=1, device_id={"dp": peer}, device_id_type=MESH)
    pl.semaphore_wait(barrier, 4)

    rows_in = key_ref.shape[0]
    sources = (key_ref, value_ref)
    outs = (key_out, value_out)

    def rows_of(index):
        return pl.ds(pl.multiple_of(index * rows_in, rows_in), rows_in)

    def send(w, src, block, sems, e, peer):
        copy = pltpu.make_async_remote_copy(
            src_ref=src,
            dst_ref=outs[w].at[rows_of(block)],
            send_sem=sems[0].at[e],
            recv_sem=sems[1].at[e],
            device_id={"dp": peer},
            device_id_type=MESH,
        )
        copy.start()
        return copy

    y_sems, x_sems, c_sems = (y_send, y_recv), (x_send, x_recv), (c_send, c_recv)
    steps = {(0, 0): 4, (0, 1): 3, (1, 0): 3, (1, 1): 4}
    event = {}
    for s in range(1, 5):
        for p, w in ((0, 0), (0, 1), (1, 0)):
            for d in range(2):
                if s <= steps[(w, d)]:
                    event[(s, p, w, d)] = len(event)
    late = {}
    for s in range(1, 5):
        for d in range(2):
            if s <= steps[(1, d)]:
                late[(s, d)] = len(late)
    y_copies, x_copies, c_copies = {}, {}, {}

    for w in range(2):
        x_copies[w] = send(w, sources[w], dp, x_sems, w, x_partner)
    for w in range(2):
        for d in range(2):
            e = event[(1, 0, w, d)]
            y_copies[e] = send(w, sources[w], dp, y_sems, e, ups[d])
    for w in range(2):
        c_copies[w] = send(w, sources[w], dp, c_sems, w, c_partner)
    own = []
    for w in range(2):
        copy = pltpu.make_async_copy(sources[w], outs[w].at[rows_of(dp)], own_sem.at[w])
        copy.start()
        own.append(copy)
    def hidden_rows(x, c):
        size = hidden_ref.shape[0]
        return hidden_out.at[pl.ds(pl.multiple_of((x * 2 + c) * size, size), size)]

    def send_hidden(src, dst, e, peer):
        copy = pltpu.make_async_remote_copy(
            src_ref=src,
            dst_ref=dst,
            send_sem=h_send.at[e],
            recv_sem=h_recv.at[e],
            device_id={"dp": peer},
            device_id_type=MESH,
        )
        copy.start()
        return copy

    hidden_x = send_hidden(hidden_ref, hidden_rows(x_pos, core), 0, x_partner)
    hidden_c = send_hidden(hidden_ref, hidden_rows(x_pos, core), 1, c_partner)
    copy = pltpu.make_async_copy(hidden_ref, hidden_rows(x_pos, core), own_sem.at[2])
    copy.start()
    own.append(copy)
    for w in range(2):
        x_copies[w].wait_recv()
        view = outs[w].at[rows_of(x_partner)]
        if w == 0:
            for d in range(2):
                e = event[(1, 1, w, d)]
                y_copies[e] = send(w, view, x_partner, y_sems, e, ups[d])
        c_copies[2 + w] = send(w, view, x_partner, c_sems, 2 + w, c_partner)

    def near(s, d):
        return y_pos - s if d == 0 else y_pos + s

    def take_late(s):
        for d in range(2):
            if (s, d) in late:
                e = late[(s, d)]
                block = place(other_x, near(s, d), core)
                x_copies[2 + e].wait_recv()
                view = outs[1].at[rows_of(block)]
                n = 4 + len(event) + e
                c_copies[n] = send(1, view, block, c_sems, n, c_partner)

    for s in range(1, 5):
        for (step, p, w, d), e in event.items():
            if step != s:
                continue
            block = place(x_pos if p == 0 else other_x, near(s, d), core)
            y_copies[e].wait_recv()
            view = outs[w].at[rows_of(block)]
            if s < steps[(w, d)]:
                n = event[(s + 1, p, w, d)]
                y_copies[n] = send(w, view, block, y_sems, n, ups[d])
            if w == 1:
                n = 2 + late[(s, d)]
                x_copies[n] = send(w, view, block, x_sems, n, x_partner)
            c_copies[4 + e] = send(w, view, block, c_sems, 4 + e, c_partner)
        if s > 1:
            take_late(s - 1)
    take_late(4)
    hidden_x.wait_recv()
    far = hidden_rows(other_x, core)
    hidden_d = send_hidden(far, far, 2, c_partner)
    for copy in own:
        copy.wait()
    for copy in x_copies.values():
        copy.wait_send()
    for copy in y_copies.values():
        copy.wait_send()
    for copy in c_copies.values():
        copy.wait()
    hidden_x.wait_send()
    hidden_c.wait()
    hidden_d.wait()


def gather_up(key_up, value_up, hidden, dp_size):
    rows, cols = key_up.shape
    full = jax.ShapeDtypeStruct((rows * dp_size, cols), key_up.dtype)
    dma = pltpu.SemaphoreType.DMA
    return pl.pallas_call(
        gather_kernel,
        out_shape=(
            full, full, jax.ShapeDtypeStruct((QUAD * hidden.shape[0], hidden.shape[1]), BF16)
        ),
        in_specs=[VMEM_SPEC] * 3,
        out_specs=(VMEM_SPEC,) * 3,
        scratch_shapes=[
            dma((21,)), dma((21,)), dma((9,)), dma((9,)), dma((32,)), dma((32,)), dma((3,)),
            dma((3,)), dma((3,)),
        ],
        compiler_params=pltpu.CompilerParams(collective_id=0, has_side_effects=True),
        name="gather_up",
    )(key_up, value_up, hidden)


def dot(a, b, dims):
    return lax.dot_general(a, b, (dims, ((), ())), preferred_element_type=F32)


NN = ((1,), (0,))
NT = ((1,), (1,))
TN = ((0,), (0,))


def attention_kernel(
    scale_factor,
    latent_ref, raw_ref, gain_ref, cos_ref, sin_ref,
    query_ref, rope_ref, cot_ref, key_up_ref, value_up_ref,
    grad_query_ref, grad_rope_ref, part_ref, rope_part_ref,
    latent, key_rot, total, rope_total,
):
    step = pl.program_id(0)
    rank = latent_ref.shape[1]
    rope_width = raw_ref.shape[0]
    half = rope_width // 2

    @pl.when(step == 0)
    def _():
        x = latent_ref[...].astype(F32)
        inv = lax.rsqrt(jnp.mean(x * x, axis=1, keepdims=True) + norm_eps)
        latent[...] = (x * inv * gain_ref[...]).astype(BF16)
        raw = raw_ref[...].astype(F32)
        u, w = raw[:half], raw[half:]
        cos, sin = cos_ref[...], sin_ref[...]
        key_rot[...] = jnp.concatenate((u * cos - w * sin, u * sin + w * cos), axis=0).astype(BF16)
        total[...] = jnp.zeros_like(total)
        rope_total[...] = jnp.zeros_like(rope_total)

    tokens = latent_ref.shape[0]
    width = query_ref.shape[1] // 2
    keys2 = dot(latent[...], key_up_ref[...], NN).astype(BF16)
    values2 = dot(latent[...], value_up_ref[...], NN).astype(BF16)
    rot = key_rot[...]
    causal = lax.broadcasted_iota(jnp.int32, (tokens, tokens), 0) >= lax.broadcasted_iota(
        jnp.int32, (tokens, tokens), 1
    )
    grad_keys, grad_values, grad_ropes = [], [], []
    for h in range(2):
        cols = slice(h * width, (h + 1) * width)
        query = query_ref[:, cols]
        rope = rope_ref[:, h * rope_width : (h + 1) * rope_width]
        cot = cot_ref[:, cols]
        key = keys2[:, cols]
        value = values2[:, cols]
        scores = (dot(query, key, NT) + dot(rope, rot, NN)) * scale_factor
        scores = jnp.where(causal, scores, -1e30)
        grown = jnp.exp(scores - jnp.max(scores, axis=1, keepdims=True))
        probs = grown / jnp.sum(grown, axis=1, keepdims=True)
        prob_low = probs.astype(BF16)
        grad_probs = dot(cot, value, NT)
        delta = jnp.sum(prob_low.astype(F32) * grad_probs, axis=1, keepdims=True)
        score_low = (probs * (grad_probs - delta) * scale_factor).astype(BF16)
        grad_query_ref[:, cols] = dot(score_low, key, NN).astype(BF16)
        grad_ropes.append(dot(score_low, rot, NT).astype(BF16))
        grad_keys.append(dot(score_low, query, TN).astype(BF16))
        grad_values.append(dot(prob_low, cot, TN).astype(BF16))
        rope_total[...] += dot(score_low, rope, TN)
    grad_rope_ref[...] = jnp.concatenate(grad_ropes, axis=1)
    total[...] += dot(jnp.concatenate(grad_keys, axis=1), key_up_ref[...], NT) + dot(
        jnp.concatenate(grad_values, axis=1), value_up_ref[...], NT
    )

    @pl.when(step == pl.num_programs(0) - 1)
    def _():
        part_ref[...] = total[...]
        pairs = rope_total[...].reshape(tokens // CHUNK, 2, CHUNK // 2, rope_width)
        rope_part_ref[...] = jnp.concatenate((pairs[:, 0], pairs[:, 1]), axis=2).reshape(
            tokens // 2, 2 * rope_width
        )


def attention_back(latent_in, raw_key, gain, cos, sin, query, rope, cot, key_full, value_full):
    tokens, rank = latent_in.shape
    rope_width = raw_key.shape[0]
    heads = rope.shape[1] // rope_width
    width = query.shape[1] // heads
    whole = lambda a: pl.BlockSpec(a.shape, lambda i: (0, 0))
    cut = lambda rows, cols: pl.BlockSpec((rows, cols), lambda i: (0, i))
    scale_factor = 1.0 / math.sqrt(width + rope_width)
    return pl.pallas_call(
        functools.partial(attention_kernel, scale_factor),
        grid=(heads // 2,),
        out_shape=(
            jax.ShapeDtypeStruct(query.shape, BF16),
            jax.ShapeDtypeStruct(rope.shape, BF16),
            jax.ShapeDtypeStruct((tokens, rank), F32),
            jax.ShapeDtypeStruct((tokens // 2, 2 * rope_width), F32),
        ),
        in_specs=[
            whole(latent_in), whole(raw_key), whole(gain), whole(cos), whole(sin),
            cut(tokens, 2 * width), cut(tokens, 2 * rope_width), cut(tokens, 2 * width),
            cut(rank, 2 * width), cut(rank, 2 * width),
        ],
        out_specs=(
            cut(tokens, 2 * width),
            cut(tokens, 2 * rope_width),
            pl.BlockSpec((tokens, rank), lambda i: (0, 0)),
            pl.BlockSpec((tokens // 2, 2 * rope_width), lambda i: (0, 0)),
        ),
        scratch_shapes=[
            pltpu.VMEM((tokens, rank), BF16),
            pltpu.VMEM((rope_width, tokens), BF16),
            pltpu.VMEM((tokens, rank), F32),
            pltpu.VMEM((tokens, rope_width), F32),
        ],
        name="attention_back",
    )(latent_in, raw_key, gain, jnp.asarray(cos), jnp.asarray(sin), query, rope, cot, key_full, value_full)


def tail_tables(rows_out):
    per_quad = Y_SIZE * rows_out

    def column(member, q):
        y, r = divmod(q, rows_out)
        return (((member // 2) * Y_SIZE + y) * 2 + member % 2) * rows_out + r

    extra = per_quad - 128
    order = np.full((1, (QUAD + 1) * 128), -1, np.int32)
    for member in range(QUAD):
        for q in range(per_quad):
            lane = member * 128 + q if q < 128 else QUAD * 128 + member * extra + q - 128
            order[0, lane] = column(member, q)
    rows = np.full((Y_SIZE * SLOT, 1), -1000, np.int32)
    for y in range(Y_SIZE):
        rows[y * SLOT : y * SLOT + rows_out, 0] = y * rows_out + np.arange(rows_out)
    return order, rows


def tail_kernel(
    part_ref, rope_part_ref, latent_ref, gain_ref, cos_ref, sin_ref, hidden_ref, order_ref,
    rows_ref, out_ref, sum_recv, rope_recv, kv_own, quad_out, quad_in, block_out, block_all, y_out, y_in,
    s1, r1, s2, r2, s3, r3, s4, r4, s5, r5,
):
    dp = lax.axis_index("dp")
    head = lax.axis_index("head")
    core = lax.rem(dp, 2)
    chip = dp // 2
    y_pos = lax.rem(chip, Y_SIZE)
    x_pos = chip // Y_SIZE
    member = x_pos * 2 + core
    rank = latent_ref.shape[1]
    tokens = latent_ref.shape[0]
    rope_width = 2 * cos_ref.shape[1]
    half = rope_width // 2
    rows_out = out_ref.shape[0]
    kv_width = rank + rope_width
    extra = Y_SIZE * rows_out - 128

    def head_peer(k):
        return lax.rem(head + k, HEAD_RANKS)

    def y_peer(k):
        return lax.rem(y_pos + k, Y_SIZE)

    def y_device(k):
        return (x_pos * Y_SIZE + y_peer(k)) * 2 + core

    def quad_peer(k):
        return lax.rem(member + k, QUAD)

    def quad_device(k):
        other = quad_peer(k)
        return ((other // 2) * Y_SIZE + y_pos) * 2 + lax.rem(other, 2)

    barrier = pltpu.get_barrier_semaphore()

    @pl.loop(1, HEAD_RANKS)
    def _(k):
        pl.semaphore_signal(barrier, inc=1, device_id={"head": head_peer(k)}, device_id_type=MESH)

    @pl.loop(1, Y_SIZE)
    def _(k):
        pl.semaphore_signal(barrier, inc=1, device_id={"dp": y_device(k)}, device_id_type=MESH)

    @pl.loop(1, QUAD)
    def _(k):
        pl.semaphore_signal(barrier, inc=1, device_id={"dp": quad_device(k)}, device_id_type=MESH)

    pl.semaphore_wait(barrier, HEAD_RANKS - 1 + Y_SIZE - 1 + QUAD - 1)

    def rows_of(index, size):
        return pl.ds(pl.multiple_of(index * size, size), size)

    def sum_copy(k):
        return pltpu.make_async_remote_copy(
            src_ref=part_ref.at[rows_of(head_peer(k), CHUNK)],
            dst_ref=sum_recv.at[k],
            send_sem=s1.at[k],
            recv_sem=r1.at[k],
            device_id={"head": head_peer(k)},
            device_id_type=MESH,
        )

    def rope_copy(k):
        return pltpu.make_async_remote_copy(
            src_ref=rope_part_ref.at[rows_of(head_peer(k), CHUNK // 2)],
            dst_ref=rope_recv.at[k],
            send_sem=s5.at[k],
            recv_sem=r5.at[k],
            device_id={"head": head_peer(k)},
            device_id_type=MESH,
        )

    @pl.loop(1, HEAD_RANKS)
    def _(k):
        sum_copy(k).start()
        rope_copy(k).start()

    mine = rows_of(head, CHUNK)
    x = latent_ref[mine, :].astype(F32)
    inv = lax.rsqrt(jnp.mean(x * x, axis=1, keepdims=True) + norm_eps)
    cos, sin = cos_ref[mine, :], sin_ref[mine, :]
    total = part_ref[mine, :]
    rope_sum = rope_part_ref[rows_of(head, CHUNK // 2), :]
    iota = lax.broadcasted_iota(jnp.int32, (LANES, LANES), 0)
    select = jnp.where(iota == order_ref[...], 1.0, 0.0).astype(BF16)

    @pl.loop(1, HEAD_RANKS)
    def _(k):
        sum_copy(k).wait()
        rope_copy(k).wait()

    for k in range(1, HEAD_RANKS):
        total += sum_recv[k]
        rope_sum += rope_recv[k]
    scaled = gain_ref[...] * total
    inner = jnp.sum(x * scaled, axis=1, keepdims=True)
    latent_grad = inv * scaled - x * (inv * inv * inv) * inner / rank
    rope_sum = jnp.concatenate((rope_sum[:, :rope_width], rope_sum[:, rope_width:]), axis=0)
    g, q = rope_sum[:, :half], rope_sum[:, half:]
    rope_grad = jnp.concatenate(
        (
            g * cos + q * sin,
            q * cos - g * sin,
            jnp.zeros((CHUNK, LANES - kv_width), F32),
        ),
        axis=1,
    )
    kv_own[:, :rank] = latent_grad.astype(BF16)
    kv_own[:, rank:] = rope_grad.astype(BF16)

    sent = dot(kv_own[...], select, NN).astype(BF16)
    for m in range(QUAD):
        quad_out[m, 0] = sent[:, m * 128 : (m + 1) * 128]
        quad_out[m, 1] = sent[:, QUAD * 128 :]

    def quad_copy(k):
        return pltpu.make_async_remote_copy(
            src_ref=quad_out.at[quad_peer(k)],
            dst_ref=quad_in.at[member],
            send_sem=s2.at[k],
            recv_sem=r2.at[k],
            device_id={"dp": quad_device(k)},
            device_id_type=MESH,
        )

    for k in range(1, QUAD):
        quad_copy(k).start()
    quad_in[member] = quad_out[member]
    lane_in = lax.broadcasted_iota(jnp.int32, (128, 128), 0)
    lane_to = lax.broadcasted_iota(jnp.int32, (128, 128), 1)
    for k in range(1, QUAD):
        quad_copy(k).wait()
    rest = jnp.zeros((CHUNK, 128), F32)
    for m in range(QUAD):
        block_out[m] = quad_in[m, 0]
        inside = (lane_to >= m * extra) & (lane_to < (m + 1) * extra)
        move = inside & (lane_in - member * extra == lane_to - m * extra)
        rest += dot(quad_in[m, 1], jnp.where(move, 1.0, 0.0).astype(BF16), NN)
    block_out[QUAD] = rest.astype(BF16)

    def block_copy(k):
        return pltpu.make_async_remote_copy(
            src_ref=block_out,
            dst_ref=block_all.at[:, mine],
            send_sem=s3.at[k],
            recv_sem=r3.at[k],
            device_id={"head": head_peer(k)},
            device_id_type=MESH,
        )

    @pl.loop(1, HEAD_RANKS)
    def _(k):
        block_copy(k).start()

    block_all[:, mine, :] = block_out[...]
    q_row = rows_ref[...]
    lane = lax.broadcasted_iota(jnp.int32, (Y_SIZE * SLOT, 128), 1)
    pick = jnp.where(lane == q_row, 1.0, 0.0).astype(BF16)
    q_rest = jnp.where(q_row >= 128, q_row - 128, -1000)
    pick_rest = [
        jnp.where(lane == q_rest + m * extra, 1.0, 0.0).astype(BF16) for m in range(QUAD)
    ]

    @pl.loop(1, HEAD_RANKS)
    def _(k):
        block_copy(k).wait()

    cols = out_ref.shape[1]
    grad = jnp.zeros((Y_SIZE * SLOT, cols), F32)
    for m in range(QUAD):
        picked = dot(pick, block_all[m], NT) + dot(pick_rest[m], block_all[QUAD], NT)
        grad += dot(
            picked.astype(BF16), hidden_ref[m * cols : (m + 1) * cols, :], NT
        )
    full = cols // 128
    rest_rows = rows_out // 2
    y_out[...] = jnp.zeros_like(y_out)
    for y in range(Y_SIZE):
        piece = grad[y * SLOT : y * SLOT + rows_out]
        for t in range(full):
            y_out[y, t * rows_out : (t + 1) * rows_out, :] = piece[:, t * 128 : (t + 1) * 128]
        edge = piece[:, full * 128 :]
        y_out[y, full * rows_out : full * rows_out + rest_rows, :] = jnp.concatenate(
            (edge[:rest_rows], edge[rest_rows:]), axis=1
        )

    def y_copy(k):
        return pltpu.make_async_remote_copy(
            src_ref=y_out.at[y_peer(k)],
            dst_ref=y_in.at[k],
            send_sem=s4.at[k],
            recv_sem=r4.at[k],
            device_id={"dp": y_device(k)},
            device_id_type=MESH,
        )

    @pl.loop(1, Y_SIZE)
    def _(k):
        y_copy(k).start()

    first = y_out[y_pos]

    @pl.loop(1, Y_SIZE)
    def _(k):
        y_copy(k).wait()

    for k in range(1, Y_SIZE):
        first += y_in[k]
    for t in range(full):
        out_ref[:, t * 128 : (t + 1) * 128] = first[t * rows_out : (t + 1) * rows_out]
    edge = first[full * rows_out : full * rows_out + rest_rows]
    out_ref[:rest_rows, full * 128 :] = edge[:, :64]
    out_ref[rest_rows:, full * 128 :] = edge[:, 64:]


def tail(part, rope_part, latent_in, gain, cos, sin, hidden_quad, rows_out):
    tokens = latent_in.shape[0]
    cols = hidden_quad.shape[0] // QUAD
    dma = pltpu.SemaphoreType.DMA
    order, rows = tail_tables(rows_out)
    return pl.pallas_call(
        tail_kernel,
        out_shape=jax.ShapeDtypeStruct((rows_out, cols), F32),
        in_specs=[VMEM_SPEC] * 9,
        out_specs=VMEM_SPEC,
        scratch_shapes=[
            pltpu.VMEM((HEAD_RANKS, CHUNK, latent_in.shape[1]), F32),
            pltpu.VMEM((HEAD_RANKS, CHUNK // 2, 128), F32),
            pltpu.VMEM((CHUNK, LANES), BF16),
            pltpu.VMEM((QUAD, 2, CHUNK, 128), BF16),
            pltpu.VMEM((QUAD, 2, CHUNK, 128), BF16),
            pltpu.VMEM((QUAD + 1, CHUNK, 128), BF16),
            pltpu.VMEM((QUAD + 1, tokens, 128), BF16),
            pltpu.VMEM((Y_SIZE, PACKED, 128), F32),
            pltpu.VMEM((Y_SIZE, PACKED, 128), F32),
            dma((HEAD_RANKS,)), dma((HEAD_RANKS,)), dma((QUAD,)), dma((QUAD,)),
            dma((HEAD_RANKS,)), dma((HEAD_RANKS,)), dma((Y_SIZE,)), dma((Y_SIZE,)),
            dma((HEAD_RANKS,)), dma((HEAD_RANKS,)),
        ],
        compiler_params=pltpu.CompilerParams(collective_id=1, has_side_effects=True),
        name="tail",
    )(part, rope_part, latent_in, gain, jnp.asarray(cos), jnp.asarray(sin), hidden_quad, jnp.asarray(order), jnp.asarray(rows))


def local(
    hidden_in,
    latent_unnormed,
    unrotated_key,
    latent_norm_scale,
    plain_query_rows,
    rotated_query_rows,
    key_up_matrix,
    value_up_matrix,
    output_cotangent,
    down_weight,
    first_moment,
    second_moment,
):
    row_count = latent_unnormed.shape[0]
    dp_size = lax.axis_size("dp")
    cos, sin = angle_tables(unrotated_key.shape[1])
    gain = latent_norm_scale[None, :]
    key_full, value_full, hidden_quad = gather_up(
        key_up_matrix, value_up_matrix, hidden_in.T, dp_size
    )
    grad_query, grad_rope, part, rope_part = attention_back(
        latent_unnormed, unrotated_key.T, gain, cos.T, sin.T,
        plain_query_rows, rotated_query_rows, output_cotangent, key_full, value_full,
    )
    weight_sum = tail(
        part, rope_part, latent_unnormed, gain, cos, sin, hidden_quad, down_weight.shape[0]
    )
    weight_grad = weight_sum / (row_count * dp_size)
    new_first = beta_one * first_moment + (1.0 - beta_one) * weight_grad
    new_second = beta_two * second_moment + (1.0 - beta_two) * weight_grad * weight_grad
    direction = new_first / bias_one / (jnp.sqrt(new_second / bias_two) + adam_eps)
    new_weight = down_weight - learn_rate * (direction + decay_rate * down_weight)
    return grad_query, grad_rope, new_weight, new_first, new_second


def solution(mesh):
    placed = (
        P("dp", "head"),
        P("dp", None),
        P("dp", None),
        P(),
        P("dp", "head"),
        P("dp", "head"),
        P("dp", "head"),
        P("dp", "head"),
        P("dp", "head"),
        P("dp", "head"),
        P("dp", "head"),
        P("dp", "head"),
    )
    return jax.shard_map(
        local,
        mesh=mesh,
        in_specs=placed,
        out_specs=(
            P("dp", "head"),
            P("dp", "head"),
            P("dp", "head"),
            P("dp", "head"),
            P("dp", "head"),
        ),
        check_vma=False,
    )
```

```python
import functools
import math

import jax
import jax.numpy as jnp
import numpy as np
from jax import lax
from jax.experimental import pallas as pl
from jax.experimental.pallas import tpu as pltpu
from jax.sharding import PartitionSpec as P

SEQUENCE_LENGTH = 256

norm_eps = 1e-06
beta_one = 0.9
beta_two = 0.999
adam_eps = 1e-08
learn_rate = 0.01
decay_rate = 0.1
bias_one = 1.0 - 0.9**2
bias_two = 1.0 - 0.999**2

MESH = pl.DeviceIdType.MESH
BF16 = jnp.bfloat16
F32 = jnp.float32

Y_SIZE = 8
HEAD_RANKS = 16
LANES = 640
CHUNK = 16
SLOT = 24
PACKED = 64
QUAD = 4
VMEM_SPEC = pl.BlockSpec(memory_space=pltpu.VMEM)


def angle_tables(rope_width):
    half_width = rope_width // 2
    inverse_freq = np.exp(
        np.arange(half_width, dtype=np.float32)
        * np.float32(-2.0 * math.log(10000.0) / rope_width)
    ).astype(np.float32)
    angles = np.arange(SEQUENCE_LENGTH, dtype=np.float32)[:, None] * inverse_freq[None, :]
    return np.cos(angles).astype(np.float32), np.sin(angles).astype(np.float32)


def gather_kernel(
    key_ref, value_ref, hidden_ref, key_out, value_out, hidden_out,
    y_send, y_recv, x_send, x_recv, c_send, c_recv, own_sem, h_send, h_recv,
):
    dp = lax.axis_index("dp")
    core = lax.rem(dp, 2)
    chip = dp // 2
    y_pos = lax.rem(chip, Y_SIZE)
    x_pos = chip // Y_SIZE

    def place(x, y, c):
        return (x * Y_SIZE + lax.rem(y + Y_SIZE, Y_SIZE)) * 2 + c

    other_x = 1 - x_pos
    ups = (place(x_pos, y_pos + 1, core), place(x_pos, y_pos - 1, core))
    x_partner = place(other_x, y_pos, core)
    c_partner = place(x_pos, y_pos, 1 - core)

    barrier = pltpu.get_barrier_semaphore()
    for peer in (ups[0], ups[1], x_partner, c_partner):
        pl.semaphore_signal(barrier, inc=1, device_id={"dp": peer}, device_id_type=MESH)
    pl.semaphore_wait(barrier, 4)

    rows_in = key_ref.shape[0]
    sources = (key_ref, value_ref)
    outs = (key_out, value_out)

    def rows_of(index):
        return pl.ds(pl.multiple_of(index * rows_in, rows_in), rows_in)

    def send(w, src, block, sems, e, peer):
        copy = pltpu.make_async_remote_copy(
            src_ref=src,
            dst_ref=outs[w].at[rows_of(block)],
            send_sem=sems[0].at[e],
            recv_sem=sems[1].at[e],
            device_id={"dp": peer},
            device_id_type=MESH,
        )
        copy.start()
        return copy

    y_sems, x_sems, c_sems = (y_send, y_recv), (x_send, x_recv), (c_send, c_recv)
    steps = {(0, 0): 4, (0, 1): 3, (1, 0): 3, (1, 1): 4}
    event = {}
    for s in range(1, 5):
        for p, w in ((0, 0), (0, 1), (1, 0)):
            for d in range(2):
                if s <= steps[(w, d)]:
                    event[(s, p, w, d)] = len(event)
    late = {}
    for s in range(1, 5):
        for d in range(2):
            if s <= steps[(1, d)]:
                late[(s, d)] = len(late)
    y_copies, x_copies, c_copies = {}, {}, {}

    for w in range(2):
        x_copies[w] = send(w, sources[w], dp, x_sems, w, x_partner)
    for w in range(2):
        for d in range(2):
            e = event[(1, 0, w, d)]
            y_copies[e] = send(w, sources[w], dp, y_sems, e, ups[d])
    for w in range(2):
        c_copies[w] = send(w, sources[w], dp, c_sems, w, c_partner)
    own = []
    for w in range(2):
        copy = pltpu.make_async_copy(sources[w], outs[w].at[rows_of(dp)], own_sem.at[w])
        copy.start()
        own.append(copy)
    def hidden_rows(x, c):
        size = hidden_ref.shape[0]
        return hidden_out.at[pl.ds(pl.multiple_of((x * 2 + c) * size, size), size)]

    def send_hidden(src, dst, e, peer):
        copy = pltpu.make_async_remote_copy(
            src_ref=src,
            dst_ref=dst,
            send_sem=h_send.at[e],
            recv_sem=h_recv.at[e],
            device_id={"dp": peer},
            device_id_type=MESH,
        )
        copy.start()
        return copy

    hidden_x = send_hidden(hidden_ref, hidden_rows(x_pos, core), 0, x_partner)
    hidden_c = send_hidden(hidden_ref, hidden_rows(x_pos, core), 1, c_partner)
    copy = pltpu.make_async_copy(hidden_ref, hidden_rows(x_pos, core), own_sem.at[2])
    copy.start()
    own.append(copy)
    for w in range(2):
        x_copies[w].wait_recv()
        view = outs[w].at[rows_of(x_partner)]
        if w == 0:
            for d in range(2):
                e = event[(1, 1, w, d)]
                y_copies[e] = send(w, view, x_partner, y_sems, e, ups[d])
        c_copies[2 + w] = send(w, view, x_partner, c_sems, 2 + w, c_partner)

    def near(s, d):
        return y_pos - s if d == 0 else y_pos + s

    def take_late(s):
        for d in range(2):
            if (s, d) in late:
                e = late[(s, d)]
                block = place(other_x, near(s, d), core)
                x_copies[2 + e].wait_recv()
                view = outs[1].at[rows_of(block)]
                n = 4 + len(event) + e
                c_copies[n] = send(1, view, block, c_sems, n, c_partner)

    for s in range(1, 5):
        for (step, p, w, d), e in event.items():
            if step != s:
                continue
            block = place(x_pos if p == 0 else other_x, near(s, d), core)
            y_copies[e].wait_recv()
            view = outs[w].at[rows_of(block)]
            if s < steps[(w, d)]:
                n = event[(s + 1, p, w, d)]
                y_copies[n] = send(w, view, block, y_sems, n, ups[d])
            if w == 1:
                n = 2 + late[(s, d)]
                x_copies[n] = send(w, view, block, x_sems, n, x_partner)
            c_copies[4 + e] = send(w, view, block, c_sems, 4 + e, c_partner)
        if s > 1:
            take_late(s - 1)
    take_late(4)
    hidden_x.wait_recv()
    far = hidden_rows(other_x, core)
    hidden_d = send_hidden(far, far, 2, c_partner)
    for copy in own:
        copy.wait()
    for copy in x_copies.values():
        copy.wait_send()
    for copy in y_copies.values():
        copy.wait_send()
    for copy in c_copies.values():
        copy.wait()
    hidden_x.wait_send()
    hidden_c.wait()
    hidden_d.wait()


def gather_up(key_up, value_up, hidden, dp_size):
    rows, cols = key_up.shape
    full = jax.ShapeDtypeStruct((rows * dp_size, cols), key_up.dtype)
    dma = pltpu.SemaphoreType.DMA
    return pl.pallas_call(
        gather_kernel,
        out_shape=(
            full, full, jax.ShapeDtypeStruct((QUAD * hidden.shape[0], hidden.shape[1]), BF16)
        ),
        in_specs=[VMEM_SPEC] * 3,
        out_specs=(VMEM_SPEC,) * 3,
        scratch_shapes=[
            dma((21,)), dma((21,)), dma((9,)), dma((9,)), dma((32,)), dma((32,)), dma((3,)),
            dma((3,)), dma((3,)),
        ],
        compiler_params=pltpu.CompilerParams(collective_id=0, has_side_effects=True),
        name="gather_up",
    )(key_up, value_up, hidden)


def dot(a, b, dims):
    return lax.dot_general(a, b, (dims, ((), ())), preferred_element_type=F32)


NN = ((1,), (0,))
NT = ((1,), (1,))
TN = ((0,), (0,))


def attention_kernel(
    scale_factor,
    latent_ref, raw_ref, gain_ref, cos_ref, sin_ref,
    query_ref, rope_ref, cot_ref, key_up_ref, value_up_ref,
    grad_query_ref, grad_rope_ref, part_ref, rope_part_ref,
    latent, key_rot, total, rope_total,
):
    step = pl.program_id(0)
    rank = latent_ref.shape[1]
    rope_width = raw_ref.shape[0]
    half = rope_width // 2

    @pl.when(step == 0)
    def _():
        x = latent_ref[...].astype(F32)
        inv = lax.rsqrt(jnp.mean(x * x, axis=1, keepdims=True) + norm_eps)
        latent[...] = (x * inv * gain_ref[...]).astype(BF16)
        raw = raw_ref[...].astype(F32)
        u, w = raw[:half], raw[half:]
        cos, sin = cos_ref[...], sin_ref[...]
        rotated = jnp.concatenate((u * cos - w * sin, u * sin + w * cos), axis=0)
        key_rot[...] = rotated.T.astype(BF16)
        total[...] = jnp.zeros_like(total)
        rope_total[...] = jnp.zeros_like(rope_total)

    tokens = latent_ref.shape[0]
    width = query_ref.shape[1] // 2
    keys2 = dot(latent[...], key_up_ref[...], NN).astype(BF16)
    values2 = dot(latent[...], value_up_ref[...], NN).astype(BF16)
    rot = key_rot[...]
    causal = lax.broadcasted_iota(jnp.int32, (tokens, tokens), 0) <= lax.broadcasted_iota(
        jnp.int32, (tokens, tokens), 1
    )
    grad_keys, grad_values, grad_ropes = [], [], []
    for h in range(2):
        cols = slice(h * width, (h + 1) * width)
        query = query_ref[:, cols]
        rope = rope_ref[:, h * rope_width : (h + 1) * rope_width]
        cot = cot_ref[:, cols]
        key = keys2[:, cols]
        value = values2[:, cols]
        scores = (dot(key, query, NT) + dot(rot, rope, NT)) * scale_factor
        scores = jnp.where(causal, scores, -1e30)
        grown = jnp.exp(scores - jnp.max(scores, axis=0, keepdims=True))
        probs = grown * (1.0 / jnp.sum(grown, axis=0, keepdims=True))
        prob_low = probs.astype(BF16)
        grad_probs = dot(value, cot, NT)
        delta = jnp.sum(prob_low.astype(F32) * grad_probs, axis=0, keepdims=True)
        score_low = (probs * (grad_probs - delta) * scale_factor).astype(BF16)
        grad_query_ref[:, cols] = dot(score_low, key, TN).astype(BF16)
        grad_ropes.append(dot(score_low, rot, TN).astype(BF16))
        grad_keys.append(dot(score_low, query, NN).astype(BF16))
        grad_values.append(dot(prob_low, cot, NN).astype(BF16))
        rope_total[...] += dot(score_low, rope, NN)
    grad_rope_ref[...] = jnp.concatenate(grad_ropes, axis=1)
    total[...] += dot(jnp.concatenate(grad_keys, axis=1), key_up_ref[...], NT) + dot(
        jnp.concatenate(grad_values, axis=1), value_up_ref[...], NT
    )

    @pl.when(step == pl.num_programs(0) - 1)
    def _():
        part_ref[...] = total[...]
        pairs = rope_total[...].reshape(tokens // CHUNK, 2, CHUNK // 2, rope_width)
        rope_part_ref[...] = jnp.concatenate((pairs[:, 0], pairs[:, 1]), axis=2).reshape(
            tokens // 2, 2 * rope_width
        )


def attention_back(latent_in, raw_key, gain, cos, sin, query, rope, cot, key_full, value_full):
    tokens, rank = latent_in.shape
    rope_width = raw_key.shape[0]
    heads = rope.shape[1] // rope_width
    width = query.shape[1] // heads
    whole = lambda a: pl.BlockSpec(a.shape, lambda i: (0, 0))
    cut = lambda rows, cols: pl.BlockSpec((rows, cols), lambda i: (0, i))
    scale_factor = 1.0 / math.sqrt(width + rope_width)
    return pl.pallas_call(
        functools.partial(attention_kernel, scale_factor),
        grid=(heads // 2,),
        out_shape=(
            jax.ShapeDtypeStruct(query.shape, BF16),
            jax.ShapeDtypeStruct(rope.shape, BF16),
            jax.ShapeDtypeStruct((tokens, rank), F32),
            jax.ShapeDtypeStruct((tokens // 2, 2 * rope_width), F32),
        ),
        in_specs=[
            whole(latent_in), whole(raw_key), whole(gain), whole(cos), whole(sin),
            cut(tokens, 2 * width), cut(tokens, 2 * rope_width), cut(tokens, 2 * width),
            cut(rank, 2 * width), cut(rank, 2 * width),
        ],
        out_specs=(
            cut(tokens, 2 * width),
            cut(tokens, 2 * rope_width),
            pl.BlockSpec((tokens, rank), lambda i: (0, 0)),
            pl.BlockSpec((tokens // 2, 2 * rope_width), lambda i: (0, 0)),
        ),
        scratch_shapes=[
            pltpu.VMEM((tokens, rank), BF16),
            pltpu.VMEM((tokens, rope_width), BF16),
            pltpu.VMEM((tokens, rank), F32),
            pltpu.VMEM((tokens, rope_width), F32),
        ],
        name="attention_back",
    )(latent_in, raw_key, gain, jnp.asarray(cos), jnp.asarray(sin), query, rope, cot, key_full, value_full)


def tail_tables(rows_out):
    per_quad = Y_SIZE * rows_out

    def column(member, q):
        y, r = divmod(q, rows_out)
        return (((member // 2) * Y_SIZE + y) * 2 + member % 2) * rows_out + r

    extra = per_quad - 128
    order = np.full((1, (QUAD + 1) * 128), -1, np.int32)
    for member in range(QUAD):
        for q in range(per_quad):
            lane = member * 128 + q if q < 128 else QUAD * 128 + member * extra + q - 128
            order[0, lane] = column(member, q)
    rows = np.full((Y_SIZE * SLOT, 1), -1000, np.int32)
    for y in range(Y_SIZE):
        rows[y * SLOT : y * SLOT + rows_out, 0] = y * rows_out + np.arange(rows_out)
    return order, rows


def far_first(i, size):
    return size // 2 + (1 - 2 * lax.rem(i, 2)) * ((i + 1) // 2)


def tail_kernel(
    part_ref, rope_part_ref, latent_ref, gain_ref, cos_ref, sin_ref, hidden_ref, order_ref,
    rows_ref, out_ref, sum_recv, rope_recv, kv_own, quad_out, quad_in, block_out, block_all, y_out, y_in,
    s1, r1, s2, r2, s3, r3, s4, r4, s5, r5,
):
    dp = lax.axis_index("dp")
    head = lax.axis_index("head")
    core = lax.rem(dp, 2)
    chip = dp // 2
    y_pos = lax.rem(chip, Y_SIZE)
    x_pos = chip // Y_SIZE
    member = x_pos * 2 + core
    rank = latent_ref.shape[1]
    tokens = latent_ref.shape[0]
    rope_width = 2 * cos_ref.shape[1]
    half = rope_width // 2
    rows_out = out_ref.shape[0]
    kv_width = rank + rope_width
    extra = Y_SIZE * rows_out - 128

    def head_peer(k):
        return lax.rem(head + k, HEAD_RANKS)

    def y_peer(k):
        return lax.rem(y_pos + k, Y_SIZE)

    def y_device(k):
        return (x_pos * Y_SIZE + y_peer(k)) * 2 + core

    def quad_peer(k):
        return lax.rem(member + k, QUAD)

    def quad_device(k):
        other = quad_peer(k)
        return ((other // 2) * Y_SIZE + y_pos) * 2 + lax.rem(other, 2)

    barrier = pltpu.get_barrier_semaphore()

    @pl.loop(1, HEAD_RANKS)
    def _(k):
        pl.semaphore_signal(barrier, inc=1, device_id={"head": head_peer(k)}, device_id_type=MESH)

    @pl.loop(1, Y_SIZE)
    def _(k):
        pl.semaphore_signal(barrier, inc=1, device_id={"dp": y_device(k)}, device_id_type=MESH)

    @pl.loop(1, QUAD)
    def _(k):
        pl.semaphore_signal(barrier, inc=1, device_id={"dp": quad_device(k)}, device_id_type=MESH)

    pl.semaphore_wait(barrier, HEAD_RANKS - 1 + Y_SIZE - 1 + QUAD - 1)

    def rows_of(index, size):
        return pl.ds(pl.multiple_of(index * size, size), size)

    def sum_copy(k):
        return pltpu.make_async_remote_copy(
            src_ref=part_ref.at[rows_of(head_peer(k), CHUNK)],
            dst_ref=sum_recv.at[k],
            send_sem=s1.at[k],
            recv_sem=r1.at[k],
            device_id={"head": head_peer(k)},
            device_id_type=MESH,
        )

    def rope_copy(k):
        return pltpu.make_async_remote_copy(
            src_ref=rope_part_ref.at[rows_of(head_peer(k), CHUNK // 2)],
            dst_ref=rope_recv.at[k],
            send_sem=s5.at[k],
            recv_sem=r5.at[k],
            device_id={"head": head_peer(k)},
            device_id_type=MESH,
        )

    @pl.loop(0, HEAD_RANKS - 1)
    def _(i):
        k = far_first(i, HEAD_RANKS)
        sum_copy(k).start()
        rope_copy(k).start()

    mine = rows_of(head, CHUNK)
    x = latent_ref[mine, :].astype(F32)
    inv = lax.rsqrt(jnp.mean(x * x, axis=1, keepdims=True) + norm_eps)
    cos, sin = cos_ref[mine, :], sin_ref[mine, :]
    total = part_ref[mine, :]
    rope_sum = rope_part_ref[rows_of(head, CHUNK // 2), :]
    iota = lax.broadcasted_iota(jnp.int32, (LANES, LANES), 0)
    select = jnp.where(iota == order_ref[...], 1.0, 0.0).astype(BF16)

    @pl.loop(1, HEAD_RANKS)
    def _(k):
        sum_copy(k).wait()
        rope_copy(k).wait()

    for k in range(1, HEAD_RANKS):
        total += sum_recv[k]
        rope_sum += rope_recv[k]
    scaled = gain_ref[...] * total
    inner = jnp.sum(x * scaled, axis=1, keepdims=True)
    latent_grad = inv * scaled - x * (inv * inv * inv) * inner / rank
    rope_sum = jnp.concatenate((rope_sum[:, :rope_width], rope_sum[:, rope_width:]), axis=0)
    g, q = rope_sum[:, :half], rope_sum[:, half:]
    rope_grad = jnp.concatenate(
        (
            g * cos + q * sin,
            q * cos - g * sin,
            jnp.zeros((CHUNK, LANES - kv_width), F32),
        ),
        axis=1,
    )
    kv_own[:, :rank] = latent_grad.astype(BF16)
    kv_own[:, rank:] = rope_grad.astype(BF16)

    sent = dot(kv_own[...], select, NN).astype(BF16)
    for m in range(QUAD):
        quad_out[m, 0] = sent[:, m * 128 : (m + 1) * 128]
        quad_out[m, 1] = sent[:, QUAD * 128 :]

    def quad_copy(k):
        return pltpu.make_async_remote_copy(
            src_ref=quad_out.at[quad_peer(k)],
            dst_ref=quad_in.at[member],
            send_sem=s2.at[k],
            recv_sem=r2.at[k],
            device_id={"dp": quad_device(k)},
            device_id_type=MESH,
        )

    for k in range(1, QUAD):
        quad_copy(k).start()
    quad_in[member] = quad_out[member]
    lane_in = lax.broadcasted_iota(jnp.int32, (128, 128), 0)
    lane_to = lax.broadcasted_iota(jnp.int32, (128, 128), 1)
    for k in range(1, QUAD):
        quad_copy(k).wait()
    rest = jnp.zeros((CHUNK, 128), F32)
    for m in range(QUAD):
        block_out[m] = quad_in[m, 0]
        inside = (lane_to >= m * extra) & (lane_to < (m + 1) * extra)
        move = inside & (lane_in - member * extra == lane_to - m * extra)
        rest += dot(quad_in[m, 1], jnp.where(move, 1.0, 0.0).astype(BF16), NN)
    block_out[QUAD] = rest.astype(BF16)

    def block_copy(k):
        return pltpu.make_async_remote_copy(
            src_ref=block_out,
            dst_ref=block_all.at[:, mine],
            send_sem=s3.at[k],
            recv_sem=r3.at[k],
            device_id={"head": head_peer(k)},
            device_id_type=MESH,
        )

    @pl.loop(0, HEAD_RANKS - 1)
    def _(i):
        block_copy(far_first(i, HEAD_RANKS)).start()

    block_all[:, mine, :] = block_out[...]
    q_row = rows_ref[...]
    lane = lax.broadcasted_iota(jnp.int32, (Y_SIZE * SLOT, 128), 1)
    pick = jnp.where(lane == q_row, 1.0, 0.0).astype(BF16)
    q_rest = jnp.where(q_row >= 128, q_row - 128, -1000)
    pick_rest = [
        jnp.where(lane == q_rest + m * extra, 1.0, 0.0).astype(BF16) for m in range(QUAD)
    ]

    @pl.loop(1, HEAD_RANKS)
    def _(k):
        block_copy(k).wait()

    cols = out_ref.shape[1]
    grad = jnp.zeros((Y_SIZE * SLOT, cols), F32)
    for m in range(QUAD):
        picked = dot(pick, block_all[m], NT) + dot(pick_rest[m], block_all[QUAD], NT)
        grad += dot(
            picked.astype(BF16), hidden_ref[m * cols : (m + 1) * cols, :], NT
        )
    full = cols // 128
    rest_rows = rows_out // 2
    y_out[...] = jnp.zeros_like(y_out)
    for y in range(Y_SIZE):
        piece = grad[y * SLOT : y * SLOT + rows_out]
        for t in range(full):
            y_out[y, t * rows_out : (t + 1) * rows_out, :] = piece[:, t * 128 : (t + 1) * 128]
        edge = piece[:, full * 128 :]
        y_out[y, full * rows_out : full * rows_out + rest_rows, :] = jnp.concatenate(
            (edge[:rest_rows], edge[rest_rows:]), axis=1
        )

    def y_copy(k):
        return pltpu.make_async_remote_copy(
            src_ref=y_out.at[y_peer(k)],
            dst_ref=y_in.at[k],
            send_sem=s4.at[k],
            recv_sem=r4.at[k],
            device_id={"dp": y_device(k)},
            device_id_type=MESH,
        )

    @pl.loop(0, Y_SIZE - 1)
    def _(i):
        y_copy(far_first(i, Y_SIZE)).start()

    first = y_out[y_pos]

    @pl.loop(1, Y_SIZE)
    def _(k):
        y_copy(k).wait()

    for k in range(1, Y_SIZE):
        first += y_in[k]
    for t in range(full):
        out_ref[:, t * 128 : (t + 1) * 128] = first[t * rows_out : (t + 1) * rows_out]
    edge = first[full * rows_out : full * rows_out + rest_rows]
    out_ref[:rest_rows, full * 128 :] = edge[:, :64]
    out_ref[rest_rows:, full * 128 :] = edge[:, 64:]


def tail(part, rope_part, latent_in, gain, cos, sin, hidden_quad, rows_out):
    tokens = latent_in.shape[0]
    cols = hidden_quad.shape[0] // QUAD
    dma = pltpu.SemaphoreType.DMA
    order, rows = tail_tables(rows_out)
    return pl.pallas_call(
        tail_kernel,
        out_shape=jax.ShapeDtypeStruct((rows_out, cols), F32),
        in_specs=[VMEM_SPEC] * 9,
        out_specs=VMEM_SPEC,
        scratch_shapes=[
            pltpu.VMEM((HEAD_RANKS, CHUNK, latent_in.shape[1]), F32),
            pltpu.VMEM((HEAD_RANKS, CHUNK // 2, 128), F32),
            pltpu.VMEM((CHUNK, LANES), BF16),
            pltpu.VMEM((QUAD, 2, CHUNK, 128), BF16),
            pltpu.VMEM((QUAD, 2, CHUNK, 128), BF16),
            pltpu.VMEM((QUAD + 1, CHUNK, 128), BF16),
            pltpu.VMEM((QUAD + 1, tokens, 128), BF16),
            pltpu.VMEM((Y_SIZE, PACKED, 128), F32),
            pltpu.VMEM((Y_SIZE, PACKED, 128), F32),
            dma((HEAD_RANKS,)), dma((HEAD_RANKS,)), dma((QUAD,)), dma((QUAD,)),
            dma((HEAD_RANKS,)), dma((HEAD_RANKS,)), dma((Y_SIZE,)), dma((Y_SIZE,)),
            dma((HEAD_RANKS,)), dma((HEAD_RANKS,)),
        ],
        compiler_params=pltpu.CompilerParams(collective_id=1, has_side_effects=True),
        name="tail",
    )(part, rope_part, latent_in, gain, jnp.asarray(cos), jnp.asarray(sin), hidden_quad, jnp.asarray(order), jnp.asarray(rows))


def local(
    hidden_in,
    latent_unnormed,
    unrotated_key,
    latent_norm_scale,
    plain_query_rows,
    rotated_query_rows,
    key_up_matrix,
    value_up_matrix,
    output_cotangent,
    down_weight,
    first_moment,
    second_moment,
):
    row_count = latent_unnormed.shape[0]
    dp_size = lax.axis_size("dp")
    cos, sin = angle_tables(unrotated_key.shape[1])
    gain = latent_norm_scale[None, :]
    key_full, value_full, hidden_quad = gather_up(
        key_up_matrix, value_up_matrix, hidden_in.T, dp_size
    )
    grad_query, grad_rope, part, rope_part = attention_back(
        latent_unnormed, unrotated_key.T, gain, cos.T, sin.T,
        plain_query_rows, rotated_query_rows, output_cotangent, key_full, value_full,
    )
    weight_sum = tail(
        part, rope_part, latent_unnormed, gain, cos, sin, hidden_quad, down_weight.shape[0]
    )
    weight_grad = weight_sum / (row_count * dp_size)
    new_first = beta_one * first_moment + (1.0 - beta_one) * weight_grad
    new_second = beta_two * second_moment + (1.0 - beta_two) * weight_grad * weight_grad
    direction = new_first / bias_one / (jnp.sqrt(new_second / bias_two) + adam_eps)
    new_weight = down_weight - learn_rate * (direction + decay_rate * down_weight)
    return grad_query, grad_rope, new_weight, new_first, new_second


def solution(mesh):
    placed = (
        P("dp", "head"),
        P("dp", None),
        P("dp", None),
        P(),
        P("dp", "head"),
        P("dp", "head"),
        P("dp", "head"),
        P("dp", "head"),
        P("dp", "head"),
        P("dp", "head"),
        P("dp", "head"),
        P("dp", "head"),
    )
    return jax.shard_map(
        local,
        mesh=mesh,
        in_specs=placed,
        out_specs=(
            P("dp", "head"),
            P("dp", "head"),
            P("dp", "head"),
            P("dp", "head"),
            P("dp", "head"),
        ),
        check_vma=False,
    )
```

```python
import functools
import math

import jax
import jax.numpy as jnp
import numpy as np
from jax import lax
from jax.experimental import pallas as pl
from jax.experimental.pallas import tpu as pltpu
from jax.sharding import PartitionSpec as P

SEQUENCE_LENGTH = 256

norm_eps = 1e-06
beta_one = 0.9
beta_two = 0.999
adam_eps = 1e-08
learn_rate = 0.01
decay_rate = 0.1
bias_one = 1.0 - 0.9**2
bias_two = 1.0 - 0.999**2

MESH = pl.DeviceIdType.MESH
BF16 = jnp.bfloat16
F32 = jnp.float32

Y_SIZE = 8
HEAD_RANKS = 16
LANES = 640
CHUNK = 16
SLOT = 24
PACKED = 64
QUAD = 4
VMEM_SPEC = pl.BlockSpec(memory_space=pltpu.VMEM)


def angle_tables(rope_width):
    half_width = rope_width // 2
    inverse_freq = np.exp(
        np.arange(half_width, dtype=np.float32)
        * np.float32(-2.0 * math.log(10000.0) / rope_width)
    ).astype(np.float32)
    angles = np.arange(SEQUENCE_LENGTH, dtype=np.float32)[:, None] * inverse_freq[None, :]
    return np.cos(angles).astype(np.float32), np.sin(angles).astype(np.float32)


def gather_body(
    key_ref, value_ref, hidden_ref, key_out, value_out, hidden_out,
    y_send, y_recv, x_send, x_recv, c_send, c_recv, own_sem, h_send, h_recv,
):
    dp = lax.axis_index("dp")
    core = lax.rem(dp, 2)
    chip = dp // 2
    y_pos = lax.rem(chip, Y_SIZE)
    x_pos = chip // Y_SIZE

    def place(x, y, c):
        return (x * Y_SIZE + lax.rem(y + Y_SIZE, Y_SIZE)) * 2 + c

    other_x = 1 - x_pos
    ups = (place(x_pos, y_pos + 1, core), place(x_pos, y_pos - 1, core))
    x_partner = place(other_x, y_pos, core)
    c_partner = place(x_pos, y_pos, 1 - core)

    rows_in = key_ref.shape[0]
    sources = (key_ref, value_ref)
    outs = (key_out, value_out)

    def rows_of(index):
        return pl.ds(pl.multiple_of(index * rows_in, rows_in), rows_in)

    def send(w, src, block, sems, e, peer):
        copy = pltpu.make_async_remote_copy(
            src_ref=src,
            dst_ref=outs[w].at[rows_of(block)],
            send_sem=sems[0].at[e],
            recv_sem=sems[1].at[e],
            device_id={"dp": peer},
            device_id_type=MESH,
        )
        copy.start()
        return copy

    y_sems, x_sems, c_sems = (y_send, y_recv), (x_send, x_recv), (c_send, c_recv)
    steps = {(0, 0): 4, (0, 1): 3, (1, 0): 3, (1, 1): 4}
    event = {}
    for s in range(1, 5):
        for p, w in ((0, 0), (0, 1), (1, 0)):
            for d in range(2):
                if s <= steps[(w, d)]:
                    event[(s, p, w, d)] = len(event)
    late = {}
    for s in range(1, 5):
        for d in range(2):
            if s <= steps[(1, d)]:
                late[(s, d)] = len(late)
    y_copies, x_copies, c_copies = {}, {}, {}

    for w in range(2):
        x_copies[w] = send(w, sources[w], dp, x_sems, w, x_partner)
    for w in range(2):
        for d in range(2):
            e = event[(1, 0, w, d)]
            y_copies[e] = send(w, sources[w], dp, y_sems, e, ups[d])
    for w in range(2):
        c_copies[w] = send(w, sources[w], dp, c_sems, w, c_partner)
    own = []
    for w in range(2):
        copy = pltpu.make_async_copy(sources[w], outs[w].at[rows_of(dp)], own_sem.at[w])
        copy.start()
        own.append(copy)
    def hidden_rows(x, c):
        size = hidden_ref.shape[0]
        return hidden_out.at[pl.ds(pl.multiple_of((x * 2 + c) * size, size), size)]

    def send_hidden(src, dst, e, peer):
        copy = pltpu.make_async_remote_copy(
            src_ref=src,
            dst_ref=dst,
            send_sem=h_send.at[e],
            recv_sem=h_recv.at[e],
            device_id={"dp": peer},
            device_id_type=MESH,
        )
        copy.start()
        return copy

    hidden_x = send_hidden(hidden_ref, hidden_rows(x_pos, core), 0, x_partner)
    hidden_c = send_hidden(hidden_ref, hidden_rows(x_pos, core), 1, c_partner)
    copy = pltpu.make_async_copy(hidden_ref, hidden_rows(x_pos, core), own_sem.at[2])
    copy.start()
    own.append(copy)
    for w in range(2):
        x_copies[w].wait_recv()
        view = outs[w].at[rows_of(x_partner)]
        if w == 0:
            for d in range(2):
                e = event[(1, 1, w, d)]
                y_copies[e] = send(w, view, x_partner, y_sems, e, ups[d])
        c_copies[2 + w] = send(w, view, x_partner, c_sems, 2 + w, c_partner)

    def near(s, d):
        return y_pos - s if d == 0 else y_pos + s

    def take_late(s):
        for d in range(2):
            if (s, d) in late:
                e = late[(s, d)]
                block = place(other_x, near(s, d), core)
                x_copies[2 + e].wait_recv()
                view = outs[1].at[rows_of(block)]
                n = 4 + len(event) + e
                c_copies[n] = send(1, view, block, c_sems, n, c_partner)

    for s in range(1, 5):
        for (step, p, w, d), e in event.items():
            if step != s:
                continue
            block = place(x_pos if p == 0 else other_x, near(s, d), core)
            y_copies[e].wait_recv()
            view = outs[w].at[rows_of(block)]
            if s < steps[(w, d)]:
                n = event[(s + 1, p, w, d)]
                y_copies[n] = send(w, view, block, y_sems, n, ups[d])
            if w == 1:
                n = 2 + late[(s, d)]
                x_copies[n] = send(w, view, block, x_sems, n, x_partner)
            c_copies[4 + e] = send(w, view, block, c_sems, 4 + e, c_partner)
        if s > 1:
            take_late(s - 1)
    take_late(4)
    hidden_x.wait_recv()
    far = hidden_rows(other_x, core)
    hidden_d = send_hidden(far, far, 2, c_partner)
    for copy in own:
        copy.wait()
    for copy in c_copies.values():
        copy.wait_recv()

    def finish():
        for group in (x_copies, y_copies, c_copies):
            for copy in group.values():
                copy.wait_send()
        hidden_x.wait_send()
        hidden_c.wait()
        hidden_d.wait()

    return finish


def dot(a, b, dims):
    return lax.dot_general(a, b, (dims, ((), ())), preferred_element_type=F32)


NN = ((1,), (0,))
NT = ((1,), (1,))
TN = ((0,), (0,))


def attention_start(latent_ref, raw_ref, gain_ref, cos_ref, sin_ref, latent, key_rot, total, rope_total):
    half = raw_ref.shape[0] // 2
    x = latent_ref[...].astype(F32)
    inv = lax.rsqrt(jnp.mean(x * x, axis=1, keepdims=True) + norm_eps)
    latent[...] = (x * inv * gain_ref[...]).astype(BF16)
    raw = raw_ref[...].astype(F32)
    u, w = raw[:half], raw[half:]
    cos, sin = cos_ref[...], sin_ref[...]
    rotated = jnp.concatenate((u * cos - w * sin, u * sin + w * cos), axis=0)
    key_rot[...] = rotated.T.astype(BF16)
    total[...] = jnp.zeros_like(total)
    rope_total[...] = jnp.zeros_like(rope_total)


def attention_pair(
    scale_factor, width, pair,
    query_ref, rope_ref, cot_ref, key_up_ref, value_up_ref, grad_query_ref, grad_rope_ref,
    latent, key_rot, total, rope_total,
):
    tokens = latent.shape[0]
    rope_width = key_rot.shape[1]

    def columns(size):
        return pl.ds(pl.multiple_of(pair * size, size), size)

    both = columns(2 * width)
    key_up, value_up = key_up_ref[:, both], value_up_ref[:, both]
    queries, cots = query_ref[:, both], cot_ref[:, both]
    ropes = rope_ref[:, columns(2 * rope_width)]
    keys2 = dot(latent[...], key_up, NN).astype(BF16)
    values2 = dot(latent[...], value_up, NN).astype(BF16)
    rot = key_rot[...]
    causal = lax.broadcasted_iota(jnp.int32, (tokens, tokens), 0) <= lax.broadcasted_iota(
        jnp.int32, (tokens, tokens), 1
    )
    grad_queries, grad_keys, grad_values, grad_ropes = [], [], [], []
    for h in range(2):
        cols = slice(h * width, (h + 1) * width)
        query = queries[:, cols]
        rope = ropes[:, h * rope_width : (h + 1) * rope_width]
        cot = cots[:, cols]
        key = keys2[:, cols]
        value = values2[:, cols]
        scores = (dot(key, query, NT) + dot(rot, rope, NT)) * scale_factor
        scores = jnp.where(causal, scores, -1e30)
        grown = jnp.exp(scores - jnp.max(scores, axis=0, keepdims=True))
        probs = grown * (1.0 / jnp.sum(grown, axis=0, keepdims=True))
        prob_low = probs.astype(BF16)
        grad_probs = dot(value, cot, NT)
        delta = jnp.sum(prob_low.astype(F32) * grad_probs, axis=0, keepdims=True)
        score_low = (probs * (grad_probs - delta) * scale_factor).astype(BF16)
        grad_queries.append(dot(score_low, key, TN).astype(BF16))
        grad_ropes.append(dot(score_low, rot, TN).astype(BF16))
        grad_keys.append(dot(score_low, query, NN).astype(BF16))
        grad_values.append(dot(prob_low, cot, NN).astype(BF16))
        rope_total[...] += dot(score_low, rope, NN)
    grad_query_ref[:, both] = jnp.concatenate(grad_queries, axis=1)
    grad_rope_ref[:, columns(2 * rope_width)] = jnp.concatenate(grad_ropes, axis=1)
    total[...] += dot(jnp.concatenate(grad_keys, axis=1), key_up, NT) + dot(
        jnp.concatenate(grad_values, axis=1), value_up, NT
    )


def tail_tables(rows_out):
    per_quad = Y_SIZE * rows_out

    def column(member, q):
        y, r = divmod(q, rows_out)
        return (((member // 2) * Y_SIZE + y) * 2 + member % 2) * rows_out + r

    extra = per_quad - 128
    order = np.full((1, (QUAD + 1) * 128), -1, np.int32)
    for member in range(QUAD):
        for q in range(per_quad):
            lane = member * 128 + q if q < 128 else QUAD * 128 + member * extra + q - 128
            order[0, lane] = column(member, q)
    rows = np.full((Y_SIZE * SLOT, 1), -1000, np.int32)
    for y in range(Y_SIZE):
        rows[y * SLOT : y * SLOT + rows_out, 0] = y * rows_out + np.arange(rows_out)
    return order, rows


def far_first(i, size):
    return size // 2 + (1 - 2 * lax.rem(i, 2)) * ((i + 1) // 2)


def tail_body(
    attention, part_ref, rope_part_ref, latent_ref, gain_ref, cos_ref, sin_ref, hidden_ref, order_ref,
    rows_ref, out_ref, sum_recv, rope_recv, kv_own, quad_out, quad_in, block_out, block_all, y_out, y_in,
    s1, r1, s2, r2, s3, r3, s4, r4, s5, r5,
):
    dp = lax.axis_index("dp")
    head = lax.axis_index("head")
    core = lax.rem(dp, 2)
    chip = dp // 2
    y_pos = lax.rem(chip, Y_SIZE)
    x_pos = chip // Y_SIZE
    member = x_pos * 2 + core
    rank = latent_ref.shape[1]
    tokens = latent_ref.shape[0]
    rope_width = 2 * cos_ref.shape[1]
    half = rope_width // 2
    rows_out = out_ref.shape[0]
    kv_width = rank + rope_width
    extra = Y_SIZE * rows_out - 128

    def head_peer(k):
        return lax.rem(head + k, HEAD_RANKS)

    def y_peer(k):
        return lax.rem(y_pos + k, Y_SIZE)

    def y_device(k):
        return (x_pos * Y_SIZE + y_peer(k)) * 2 + core

    def quad_peer(k):
        return lax.rem(member + k, QUAD)

    def quad_device(k):
        other = quad_peer(k)
        return ((other // 2) * Y_SIZE + y_pos) * 2 + lax.rem(other, 2)

    barrier = pltpu.get_barrier_semaphore()

    @pl.loop(1, HEAD_RANKS)
    def _(k):
        pl.semaphore_signal(barrier, inc=1, device_id={"head": head_peer(k)}, device_id_type=MESH)

    @pl.loop(1, Y_SIZE)
    def _(k):
        pl.semaphore_signal(barrier, inc=1, device_id={"dp": y_device(k)}, device_id_type=MESH)

    @pl.loop(1, QUAD)
    def _(k):
        pl.semaphore_signal(barrier, inc=1, device_id={"dp": quad_device(k)}, device_id_type=MESH)

    attention(lambda: pl.semaphore_wait(barrier, HEAD_RANKS - 1 + Y_SIZE - 1 + QUAD - 1))

    def rows_of(index, size):
        return pl.ds(pl.multiple_of(index * size, size), size)

    def sum_copy(k):
        return pltpu.make_async_remote_copy(
            src_ref=part_ref.at[rows_of(head_peer(k), CHUNK)],
            dst_ref=sum_recv.at[k],
            send_sem=s1.at[k],
            recv_sem=r1.at[k],
            device_id={"head": head_peer(k)},
            device_id_type=MESH,
        )

    def rope_copy(k):
        return pltpu.make_async_remote_copy(
            src_ref=rope_part_ref.at[rows_of(head_peer(k), CHUNK // 2)],
            dst_ref=rope_recv.at[k],
            send_sem=s5.at[k],
            recv_sem=r5.at[k],
            device_id={"head": head_peer(k)},
            device_id_type=MESH,
        )

    @pl.loop(0, HEAD_RANKS - 1)
    def _(i):
        k = far_first(i, HEAD_RANKS)
        sum_copy(k).start()
        rope_copy(k).start()

    mine = rows_of(head, CHUNK)
    x = latent_ref[mine, :].astype(F32)
    inv = lax.rsqrt(jnp.mean(x * x, axis=1, keepdims=True) + norm_eps)
    cos, sin = cos_ref[mine, :], sin_ref[mine, :]
    total = part_ref[mine, :]
    rope_sum = rope_part_ref[rows_of(head, CHUNK // 2), :]
    iota = lax.broadcasted_iota(jnp.int32, (LANES, LANES), 0)
    select = jnp.where(iota == order_ref[...], 1.0, 0.0).astype(BF16)

    @pl.loop(1, HEAD_RANKS)
    def _(k):
        sum_copy(k).wait()
        rope_copy(k).wait()

    for k in range(1, HEAD_RANKS):
        total += sum_recv[k]
        rope_sum += rope_recv[k]
    scaled = gain_ref[...] * total
    inner = jnp.sum(x * scaled, axis=1, keepdims=True)
    latent_grad = inv * scaled - x * (inv * inv * inv) * inner / rank
    rope_sum = jnp.concatenate((rope_sum[:, :rope_width], rope_sum[:, rope_width:]), axis=0)
    g, q = rope_sum[:, :half], rope_sum[:, half:]
    rope_grad = jnp.concatenate(
        (
            g * cos + q * sin,
            q * cos - g * sin,
            jnp.zeros((CHUNK, LANES - kv_width), F32),
        ),
        axis=1,
    )
    kv_own[:, :rank] = latent_grad.astype(BF16)
    kv_own[:, rank:] = rope_grad.astype(BF16)

    sent = dot(kv_own[...], select, NN).astype(BF16)
    for m in range(QUAD):
        quad_out[m, 0] = sent[:, m * 128 : (m + 1) * 128]
        quad_out[m, 1] = sent[:, QUAD * 128 :]

    def quad_copy(k):
        return pltpu.make_async_remote_copy(
            src_ref=quad_out.at[quad_peer(k)],
            dst_ref=quad_in.at[member],
            send_sem=s2.at[k],
            recv_sem=r2.at[k],
            device_id={"dp": quad_device(k)},
            device_id_type=MESH,
        )

    for k in range(1, QUAD):
        quad_copy(k).start()
    quad_in[member] = quad_out[member]
    lane_in = lax.broadcasted_iota(jnp.int32, (128, 128), 0)
    lane_to = lax.broadcasted_iota(jnp.int32, (128, 128), 1)
    for k in range(1, QUAD):
        quad_copy(k).wait()
    rest = jnp.zeros((CHUNK, 128), F32)
    for m in range(QUAD):
        block_out[m] = quad_in[m, 0]
        inside = (lane_to >= m * extra) & (lane_to < (m + 1) * extra)
        move = inside & (lane_in - member * extra == lane_to - m * extra)
        rest += dot(quad_in[m, 1], jnp.where(move, 1.0, 0.0).astype(BF16), NN)
    block_out[QUAD] = rest.astype(BF16)

    def block_copy(k):
        return pltpu.make_async_remote_copy(
            src_ref=block_out,
            dst_ref=block_all.at[:, mine],
            send_sem=s3.at[k],
            recv_sem=r3.at[k],
            device_id={"head": head_peer(k)},
            device_id_type=MESH,
        )

    @pl.loop(0, HEAD_RANKS - 1)
    def _(i):
        block_copy(far_first(i, HEAD_RANKS)).start()

    block_all[:, mine, :] = block_out[...]
    q_row = rows_ref[...]
    lane = lax.broadcasted_iota(jnp.int32, (Y_SIZE * SLOT, 128), 1)
    pick = jnp.where(lane == q_row, 1.0, 0.0).astype(BF16)
    q_rest = jnp.where(q_row >= 128, q_row - 128, -1000)
    pick_rest = [
        jnp.where(lane == q_rest + m * extra, 1.0, 0.0).astype(BF16) for m in range(QUAD)
    ]

    @pl.loop(1, HEAD_RANKS)
    def _(k):
        block_copy(k).wait()

    cols = out_ref.shape[1]
    grad = jnp.zeros((Y_SIZE * SLOT, cols), F32)
    for m in range(QUAD):
        picked = dot(pick, block_all[m], NT) + dot(pick_rest[m], block_all[QUAD], NT)
        grad += dot(
            picked.astype(BF16), hidden_ref[m * cols : (m + 1) * cols, :], NT
        )
    full = cols // 128
    rest_rows = rows_out // 2
    y_out[...] = jnp.zeros_like(y_out)
    for y in range(Y_SIZE):
        piece = grad[y * SLOT : y * SLOT + rows_out]
        for t in range(full):
            y_out[y, t * rows_out : (t + 1) * rows_out, :] = piece[:, t * 128 : (t + 1) * 128]
        edge = piece[:, full * 128 :]
        y_out[y, full * rows_out : full * rows_out + rest_rows, :] = jnp.concatenate(
            (edge[:rest_rows], edge[rest_rows:]), axis=1
        )

    def y_copy(k):
        return pltpu.make_async_remote_copy(
            src_ref=y_out.at[y_peer(k)],
            dst_ref=y_in.at[k],
            send_sem=s4.at[k],
            recv_sem=r4.at[k],
            device_id={"dp": y_device(k)},
            device_id_type=MESH,
        )

    @pl.loop(0, Y_SIZE - 1)
    def _(i):
        y_copy(far_first(i, Y_SIZE)).start()

    first = y_out[y_pos]

    @pl.loop(1, Y_SIZE)
    def _(k):
        y_copy(k).wait()

    for k in range(1, Y_SIZE):
        first += y_in[k]
    for t in range(full):
        out_ref[:, t * 128 : (t + 1) * 128] = first[t * rows_out : (t + 1) * rows_out]
    edge = first[full * rows_out : full * rows_out + rest_rows]
    out_ref[:rest_rows, full * 128 :] = edge[:, :64]
    out_ref[rest_rows:, full * 128 :] = edge[:, 64:]


def fused_kernel(scale_factor, width, count, *refs):
    refs = list(refs)

    def take(n):
        taken = refs[:n]
        del refs[:n]
        return taken

    key_in, value_in, hidden_in, latent_ref, raw_ref, gain_ref = take(6)
    cos_t, sin_t, cos_ref, sin_ref, order_ref, rows_ref = take(6)
    loads = take(3)
    grad_query_ref, grad_rope_ref, out_ref = take(3)
    key_full, value_full, hidden_quad = take(3)
    latent, key_rot, total, rope_total, rope_part = take(5)
    buffers = take(3)
    load_sem = take(1)[0]
    gather_sems = take(9)

    copies = [
        pltpu.make_async_copy(loads[n], buffers[n], load_sem.at[n]) for n in range(3)
    ]

    def attention(enter):
        for copy in copies:
            copy.start()
        attention_start(
            latent_ref, raw_ref, gain_ref, cos_t, sin_t, latent, key_rot, total, rope_total
        )
        enter()
        finish = gather_body(
            key_in, value_in, hidden_in, key_full, value_full, hidden_quad, *gather_sems
        )
        for copy in copies:
            copy.wait()

        @pl.loop(0, count)
        def _(pair):
            attention_pair(
                scale_factor, width, pair, *buffers, key_full, value_full,
                grad_query_ref, grad_rope_ref, latent, key_rot, total, rope_total,
            )

        finish()
        tokens, rope_width = rope_total.shape
        pairs = rope_total[...].reshape(tokens // CHUNK, 2, CHUNK // 2, rope_width)
        rope_part[...] = jnp.concatenate((pairs[:, 0], pairs[:, 1]), axis=2).reshape(
            tokens // 2, 2 * rope_width
        )

    tail_body(
        attention, total, rope_part, latent_ref, gain_ref, cos_ref, sin_ref, hidden_quad,
        order_ref, rows_ref, out_ref, *refs,
    )


def fused(
    key_up, value_up, hidden, latent_in, raw_key, gain, query, rope, cot, rows_out, dp_size
):
    tokens, rank = latent_in.shape
    cols = hidden.shape[0]
    rope_width = raw_key.shape[0]
    heads = rope.shape[1] // rope_width
    width = query.shape[1] // heads
    scale_factor = 1.0 / math.sqrt(width + rope_width)
    cos, sin = angle_tables(rope_width)
    order, rows = tail_tables(rows_out)
    dma = pltpu.SemaphoreType.DMA
    full = (key_up.shape[0] * dp_size, key_up.shape[1])
    any_spec = pl.BlockSpec(memory_space=pl.ANY)
    return pl.pallas_call(
        functools.partial(fused_kernel, scale_factor, width, heads // 2),
        out_shape=(
            jax.ShapeDtypeStruct(query.shape, BF16),
            jax.ShapeDtypeStruct(rope.shape, BF16),
            jax.ShapeDtypeStruct((rows_out, cols), F32),
        ),
        in_specs=[VMEM_SPEC] * 12 + [any_spec] * 3,
        out_specs=(VMEM_SPEC,) * 3,
        scratch_shapes=[
            pltpu.VMEM(full, BF16),
            pltpu.VMEM(full, BF16),
            pltpu.VMEM((QUAD * cols, tokens), BF16),
            pltpu.VMEM((tokens, rank), BF16),
            pltpu.VMEM((tokens, rope_width), BF16),
            pltpu.VMEM((tokens, rank), F32),
            pltpu.VMEM((tokens, rope_width), F32),
            pltpu.VMEM((tokens // 2, 2 * rope_width), F32),
            pltpu.VMEM(query.shape, BF16),
            pltpu.VMEM(rope.shape, BF16),
            pltpu.VMEM(cot.shape, BF16),
            dma((3,)),
            dma((21,)), dma((21,)), dma((9,)), dma((9,)), dma((32,)), dma((32,)), dma((3,)),
            dma((3,)), dma((3,)),
            pltpu.VMEM((HEAD_RANKS, CHUNK, rank), F32),
            pltpu.VMEM((HEAD_RANKS, CHUNK // 2, 128), F32),
            pltpu.VMEM((CHUNK, LANES), BF16),
            pltpu.VMEM((QUAD, 2, CHUNK, 128), BF16),
            pltpu.VMEM((QUAD, 2, CHUNK, 128), BF16),
            pltpu.VMEM((QUAD + 1, CHUNK, 128), BF16),
            pltpu.VMEM((QUAD + 1, tokens, 128), BF16),
            pltpu.VMEM((Y_SIZE, PACKED, 128), F32),
            pltpu.VMEM((Y_SIZE, PACKED, 128), F32),
            dma((HEAD_RANKS,)), dma((HEAD_RANKS,)), dma((QUAD,)), dma((QUAD,)),
            dma((HEAD_RANKS,)), dma((HEAD_RANKS,)), dma((Y_SIZE,)), dma((Y_SIZE,)),
            dma((HEAD_RANKS,)), dma((HEAD_RANKS,)),
        ],
        compiler_params=pltpu.CompilerParams(collective_id=1, has_side_effects=True),
        name="fused",
    )(
        key_up, value_up, hidden, latent_in, raw_key, gain,
        jnp.asarray(cos.T), jnp.asarray(sin.T), jnp.asarray(cos), jnp.asarray(sin),
        jnp.asarray(order), jnp.asarray(rows), query, rope, cot,
    )


def local(
    hidden_in,
    latent_unnormed,
    unrotated_key,
    latent_norm_scale,
    plain_query_rows,
    rotated_query_rows,
    key_up_matrix,
    value_up_matrix,
    output_cotangent,
    down_weight,
    first_moment,
    second_moment,
):
    row_count = latent_unnormed.shape[0]
    dp_size = lax.axis_size("dp")
    gain = latent_norm_scale[None, :]
    grad_query, grad_rope, weight_sum = fused(
        key_up_matrix, value_up_matrix, hidden_in.T, latent_unnormed, unrotated_key.T, gain,
        plain_query_rows, rotated_query_rows, output_cotangent, down_weight.shape[0], dp_size,
    )
    weight_grad = weight_sum / (row_count * dp_size)
    new_first = beta_one * first_moment + (1.0 - beta_one) * weight_grad
    new_second = beta_two * second_moment + (1.0 - beta_two) * weight_grad * weight_grad
    direction = new_first / bias_one / (jnp.sqrt(new_second / bias_two) + adam_eps)
    new_weight = down_weight - learn_rate * (direction + decay_rate * down_weight)
    return grad_query, grad_rope, new_weight, new_first, new_second


def solution(mesh):
    placed = (
        P("dp", "head"),
        P("dp", None),
        P("dp", None),
        P(),
        P("dp", "head"),
        P("dp", "head"),
        P("dp", "head"),
        P("dp", "head"),
        P("dp", "head"),
        P("dp", "head"),
        P("dp", "head"),
        P("dp", "head"),
    )
    return jax.shard_map(
        local,
        mesh=mesh,
        in_specs=placed,
        out_specs=(
            P("dp", "head"),
            P("dp", "head"),
            P("dp", "head"),
            P("dp", "head"),
            P("dp", "head"),
        ),
        check_vma=False,
    )
```

```python
import functools
import math

import jax
import jax.numpy as jnp
import numpy as np
from jax import lax
from jax.experimental import pallas as pl
from jax.experimental.pallas import tpu as pltpu
from jax.sharding import PartitionSpec as P

SEQUENCE_LENGTH = 256

norm_eps = 1e-06
beta_one = 0.9
beta_two = 0.999
adam_eps = 1e-08
learn_rate = 0.01
decay_rate = 0.1
bias_one = 1.0 - 0.9**2
bias_two = 1.0 - 0.999**2

MESH = pl.DeviceIdType.MESH
BF16 = jnp.bfloat16
F32 = jnp.float32

Y_SIZE = 8
HEAD_RANKS = 16
LANES = 640
CHUNK = 16
SLOT = 24
PACKED = 64
QUAD = 4
VMEM_SPEC = pl.BlockSpec(memory_space=pltpu.VMEM)


def angle_tables(rope_width):
    half_width = rope_width // 2
    inverse_freq = np.exp(
        np.arange(half_width, dtype=np.float32)
        * np.float32(-2.0 * math.log(10000.0) / rope_width)
    ).astype(np.float32)
    angles = np.arange(SEQUENCE_LENGTH, dtype=np.float32)[:, None] * inverse_freq[None, :]
    return np.cos(angles).astype(np.float32), np.sin(angles).astype(np.float32)


def gather_body(
    key_ref, value_ref, hidden_ref, key_out, value_out, hidden_out,
    y_send, y_recv, x_send, x_recv, c_send, c_recv, own_sem, h_send, h_recv,
):
    dp = lax.axis_index("dp")
    core = lax.rem(dp, 2)
    chip = dp // 2
    y_pos = lax.rem(chip, Y_SIZE)
    x_pos = chip // Y_SIZE

    def place(x, y, c):
        return (x * Y_SIZE + lax.rem(y + Y_SIZE, Y_SIZE)) * 2 + c

    other_x = 1 - x_pos
    ups = (place(x_pos, y_pos + 1, core), place(x_pos, y_pos - 1, core))
    x_partner = place(other_x, y_pos, core)
    c_partner = place(x_pos, y_pos, 1 - core)

    rows_in = key_ref.shape[0]
    sources = (key_ref, value_ref)
    outs = (key_out, value_out)

    def rows_of(index):
        return pl.ds(pl.multiple_of(index * rows_in, rows_in), rows_in)

    def send(w, src, block, sems, e, peer):
        copy = pltpu.make_async_remote_copy(
            src_ref=src,
            dst_ref=outs[w].at[rows_of(block)],
            send_sem=sems[0].at[e],
            recv_sem=sems[1].at[e],
            device_id={"dp": peer},
            device_id_type=MESH,
        )
        copy.start()
        return copy

    y_sems, x_sems, c_sems = (y_send, y_recv), (x_send, x_recv), (c_send, c_recv)
    steps = {(0, 0): 4, (0, 1): 3, (1, 0): 3, (1, 1): 4}
    event = {}
    for s in range(1, 5):
        for p, w in ((0, 0), (0, 1), (1, 0)):
            for d in range(2):
                if s <= steps[(w, d)]:
                    event[(s, p, w, d)] = len(event)
    late = {}
    for s in range(1, 5):
        for d in range(2):
            if s <= steps[(1, d)]:
                late[(s, d)] = len(late)
    y_copies, x_copies, c_copies = {}, {}, {}

    for w in range(2):
        x_copies[w] = send(w, sources[w], dp, x_sems, w, x_partner)
    for w in range(2):
        for d in range(2):
            e = event[(1, 0, w, d)]
            y_copies[e] = send(w, sources[w], dp, y_sems, e, ups[d])
    for w in range(2):
        c_copies[w] = send(w, sources[w], dp, c_sems, w, c_partner)
    own = []
    for w in range(2):
        copy = pltpu.make_async_copy(sources[w], outs[w].at[rows_of(dp)], own_sem.at[w])
        copy.start()
        own.append(copy)
    def hidden_rows(x, c):
        size = hidden_ref.shape[0]
        return hidden_out.at[pl.ds(pl.multiple_of((x * 2 + c) * size, size), size)]

    def send_hidden(src, dst, e, peer):
        copy = pltpu.make_async_remote_copy(
            src_ref=src,
            dst_ref=dst,
            send_sem=h_send.at[e],
            recv_sem=h_recv.at[e],
            device_id={"dp": peer},
            device_id_type=MESH,
        )
        copy.start()
        return copy

    hidden_x = send_hidden(hidden_ref, hidden_rows(x_pos, core), 0, x_partner)
    hidden_c = send_hidden(hidden_ref, hidden_rows(x_pos, core), 1, c_partner)
    copy = pltpu.make_async_copy(hidden_ref, hidden_rows(x_pos, core), own_sem.at[2])
    copy.start()
    own.append(copy)
    for w in range(2):
        x_copies[w].wait_recv()
        view = outs[w].at[rows_of(x_partner)]
        if w == 0:
            for d in range(2):
                e = event[(1, 1, w, d)]
                y_copies[e] = send(w, view, x_partner, y_sems, e, ups[d])
        c_copies[2 + w] = send(w, view, x_partner, c_sems, 2 + w, c_partner)

    def near(s, d):
        return y_pos - s if d == 0 else y_pos + s

    def take_late(s):
        for d in range(2):
            if (s, d) in late:
                e = late[(s, d)]
                block = place(other_x, near(s, d), core)
                x_copies[2 + e].wait_recv()
                view = outs[1].at[rows_of(block)]
                n = 4 + len(event) + e
                c_copies[n] = send(1, view, block, c_sems, n, c_partner)

    for s in range(1, 5):
        for (step, p, w, d), e in event.items():
            if step != s:
                continue
            block = place(x_pos if p == 0 else other_x, near(s, d), core)
            y_copies[e].wait_recv()
            view = outs[w].at[rows_of(block)]
            if s < steps[(w, d)]:
                n = event[(s + 1, p, w, d)]
                y_copies[n] = send(w, view, block, y_sems, n, ups[d])
            if w == 1:
                n = 2 + late[(s, d)]
                x_copies[n] = send(w, view, block, x_sems, n, x_partner)
            c_copies[4 + e] = send(w, view, block, c_sems, 4 + e, c_partner)
        if s > 1:
            take_late(s - 1)
    take_late(4)
    hidden_x.wait_recv()
    far = hidden_rows(other_x, core)
    hidden_d = send_hidden(far, far, 2, c_partner)
    for copy in own:
        copy.wait()
    for copy in c_copies.values():
        copy.wait_recv()

    def finish():
        for group in (x_copies, y_copies, c_copies):
            for copy in group.values():
                copy.wait_send()
        hidden_x.wait_send()
        hidden_c.wait()
        hidden_d.wait()

    return finish


def dot(a, b, dims):
    return lax.dot_general(a, b, (dims, ((), ())), preferred_element_type=F32)


NN = ((1,), (0,))
NT = ((1,), (1,))
TN = ((0,), (0,))


def attention_start(latent_ref, raw_ref, gain_ref, cos_ref, sin_ref, latent, key_rot, total, rope_total):
    half = raw_ref.shape[0] // 2
    x = latent_ref[...].astype(F32)
    inv = lax.rsqrt(jnp.mean(x * x, axis=1, keepdims=True) + norm_eps)
    latent[...] = (x * inv * gain_ref[...]).astype(BF16)
    raw = raw_ref[...].astype(F32)
    u, w = raw[:half], raw[half:]
    cos, sin = cos_ref[...], sin_ref[...]
    rotated = jnp.concatenate((u * cos - w * sin, u * sin + w * cos), axis=0)
    key_rot[...] = rotated.T.astype(BF16)
    total[...] = jnp.zeros_like(total)
    rope_total[...] = jnp.zeros_like(rope_total)


def attention_pair(
    scale_factor, width, pair,
    query_ref, rope_ref, cot_ref, key_up_ref, value_up_ref, grad_query_ref, grad_rope_ref,
    latent, key_rot, total, rope_total,
):
    tokens = latent.shape[0]
    rope_width = key_rot.shape[1]

    def columns(size):
        return slice(pair * size, (pair + 1) * size)

    both = columns(2 * width)
    key_up, value_up = key_up_ref[:, both], value_up_ref[:, both]
    queries, cots = query_ref[:, both], cot_ref[:, both]
    ropes = rope_ref[:, columns(2 * rope_width)]
    keys2 = dot(latent[...], key_up, NN).astype(BF16)
    values2 = dot(latent[...], value_up, NN).astype(BF16)
    rot = key_rot[...]
    causal = lax.broadcasted_iota(jnp.int32, (tokens, tokens), 0) <= lax.broadcasted_iota(
        jnp.int32, (tokens, tokens), 1
    )
    grad_queries, grad_keys, grad_values, grad_ropes = [], [], [], []
    for h in range(2):
        cols = slice(h * width, (h + 1) * width)
        query = queries[:, cols]
        rope = ropes[:, h * rope_width : (h + 1) * rope_width]
        cot = cots[:, cols]
        key = keys2[:, cols]
        value = values2[:, cols]
        scores = (dot(key, query, NT) + dot(rot, rope, NT)) * scale_factor
        scores = jnp.where(causal, scores, -1e30)
        grown = jnp.exp(scores - jnp.max(scores, axis=0, keepdims=True))
        probs = grown * (1.0 / jnp.sum(grown, axis=0, keepdims=True))
        prob_low = probs.astype(BF16)
        grad_probs = dot(value, cot, NT)
        delta = jnp.sum(prob_low.astype(F32) * grad_probs, axis=0, keepdims=True)
        score_low = (probs * (grad_probs - delta) * scale_factor).astype(BF16)
        grad_queries.append(dot(score_low, key, TN).astype(BF16))
        grad_ropes.append(dot(score_low, rot, TN).astype(BF16))
        grad_keys.append(dot(score_low, query, NN).astype(BF16))
        grad_values.append(dot(prob_low, cot, NN).astype(BF16))
        rope_total[...] += dot(score_low, rope, NN)
    grad_query_ref[:, both] = jnp.concatenate(grad_queries, axis=1)
    grad_rope_ref[:, columns(2 * rope_width)] = jnp.concatenate(grad_ropes, axis=1)
    total[...] += dot(jnp.concatenate(grad_keys, axis=1), key_up, NT) + dot(
        jnp.concatenate(grad_values, axis=1), value_up, NT
    )


def tail_tables(rows_out):
    per_quad = Y_SIZE * rows_out

    def column(member, q):
        y, r = divmod(q, rows_out)
        return (((member // 2) * Y_SIZE + y) * 2 + member % 2) * rows_out + r

    extra = per_quad - 128
    order = np.full((1, (QUAD + 1) * 128), -1, np.int32)
    for member in range(QUAD):
        for q in range(per_quad):
            lane = member * 128 + q if q < 128 else QUAD * 128 + member * extra + q - 128
            order[0, lane] = column(member, q)
    rows = np.full((Y_SIZE * SLOT, 1), -1000, np.int32)
    for y in range(Y_SIZE):
        rows[y * SLOT : y * SLOT + rows_out, 0] = y * rows_out + np.arange(rows_out)
    return order, rows


def far_first(i, size):
    return size // 2 + (1 - 2 * lax.rem(i, 2)) * ((i + 1) // 2)


def tail_body(
    attention, part_ref, rope_part_ref, latent_ref, gain_ref, cos_ref, sin_ref, hidden_ref, order_ref,
    rows_ref, out_ref, sum_recv, rope_recv, kv_own, quad_out, quad_in, block_out, block_all, y_out, y_in,
    s1, r1, s2, r2, s3, r3, s4, r4, s5, r5,
):
    dp = lax.axis_index("dp")
    head = lax.axis_index("head")
    core = lax.rem(dp, 2)
    chip = dp // 2
    y_pos = lax.rem(chip, Y_SIZE)
    x_pos = chip // Y_SIZE
    member = x_pos * 2 + core
    rank = latent_ref.shape[1]
    tokens = latent_ref.shape[0]
    rope_width = 2 * cos_ref.shape[1]
    half = rope_width // 2
    rows_out = out_ref.shape[0]
    kv_width = rank + rope_width
    extra = Y_SIZE * rows_out - 128

    def head_peer(k):
        return lax.rem(head + k, HEAD_RANKS)

    def y_peer(k):
        return lax.rem(y_pos + k, Y_SIZE)

    def y_device(k):
        return (x_pos * Y_SIZE + y_peer(k)) * 2 + core

    def quad_peer(k):
        return lax.rem(member + k, QUAD)

    def quad_device(k):
        other = quad_peer(k)
        return ((other // 2) * Y_SIZE + y_pos) * 2 + lax.rem(other, 2)

    barrier = pltpu.get_barrier_semaphore()

    @pl.loop(1, HEAD_RANKS)
    def _(k):
        pl.semaphore_signal(barrier, inc=1, device_id={"head": head_peer(k)}, device_id_type=MESH)

    @pl.loop(1, Y_SIZE)
    def _(k):
        pl.semaphore_signal(barrier, inc=1, device_id={"dp": y_device(k)}, device_id_type=MESH)

    @pl.loop(1, QUAD)
    def _(k):
        pl.semaphore_signal(barrier, inc=1, device_id={"dp": quad_device(k)}, device_id_type=MESH)

    attention(lambda: pl.semaphore_wait(barrier, HEAD_RANKS - 1 + Y_SIZE - 1 + QUAD - 1))

    def rows_of(index, size):
        return pl.ds(pl.multiple_of(index * size, size), size)

    def sum_copy(k):
        return pltpu.make_async_remote_copy(
            src_ref=part_ref.at[rows_of(head_peer(k), CHUNK)],
            dst_ref=sum_recv.at[k],
            send_sem=s1.at[k],
            recv_sem=r1.at[k],
            device_id={"head": head_peer(k)},
            device_id_type=MESH,
        )

    def rope_copy(k):
        return pltpu.make_async_remote_copy(
            src_ref=rope_part_ref.at[rows_of(head_peer(k), CHUNK // 2)],
            dst_ref=rope_recv.at[k],
            send_sem=s5.at[k],
            recv_sem=r5.at[k],
            device_id={"head": head_peer(k)},
            device_id_type=MESH,
        )

    @pl.loop(0, HEAD_RANKS - 1)
    def _(i):
        k = far_first(i, HEAD_RANKS)
        sum_copy(k).start()
        rope_copy(k).start()

    mine = rows_of(head, CHUNK)
    x = latent_ref[mine, :].astype(F32)
    inv = lax.rsqrt(jnp.mean(x * x, axis=1, keepdims=True) + norm_eps)
    cos, sin = cos_ref[mine, :], sin_ref[mine, :]
    total = part_ref[mine, :]
    rope_sum = rope_part_ref[rows_of(head, CHUNK // 2), :]
    iota = lax.broadcasted_iota(jnp.int32, (LANES, LANES), 0)
    select = jnp.where(iota == order_ref[...], 1.0, 0.0).astype(BF16)

    @pl.loop(1, HEAD_RANKS)
    def _(k):
        sum_copy(k).wait()
        rope_copy(k).wait()

    for k in range(1, HEAD_RANKS):
        total += sum_recv[k]
        rope_sum += rope_recv[k]
    scaled = gain_ref[...] * total
    inner = jnp.sum(x * scaled, axis=1, keepdims=True)
    latent_grad = inv * scaled - x * (inv * inv * inv) * inner / rank
    rope_sum = jnp.concatenate((rope_sum[:, :rope_width], rope_sum[:, rope_width:]), axis=0)
    g, q = rope_sum[:, :half], rope_sum[:, half:]
    rope_grad = jnp.concatenate(
        (
            g * cos + q * sin,
            q * cos - g * sin,
            jnp.zeros((CHUNK, LANES - kv_width), F32),
        ),
        axis=1,
    )
    kv_own[:, :rank] = latent_grad.astype(BF16)
    kv_own[:, rank:] = rope_grad.astype(BF16)

    sent = dot(kv_own[...], select, NN).astype(BF16)
    for m in range(QUAD):
        quad_out[m, 0] = sent[:, m * 128 : (m + 1) * 128]
        quad_out[m, 1] = sent[:, QUAD * 128 :]

    def quad_copy(k):
        return pltpu.make_async_remote_copy(
            src_ref=quad_out.at[quad_peer(k)],
            dst_ref=quad_in.at[member],
            send_sem=s2.at[k],
            recv_sem=r2.at[k],
            device_id={"dp": quad_device(k)},
            device_id_type=MESH,
        )

    for k in range(1, QUAD):
        quad_copy(k).start()
    quad_in[member] = quad_out[member]
    lane_in = lax.broadcasted_iota(jnp.int32, (128, 128), 0)
    lane_to = lax.broadcasted_iota(jnp.int32, (128, 128), 1)
    for k in range(1, QUAD):
        quad_copy(k).wait()
    rest = jnp.zeros((CHUNK, 128), F32)
    for m in range(QUAD):
        block_out[m] = quad_in[m, 0]
        inside = (lane_to >= m * extra) & (lane_to < (m + 1) * extra)
        move = inside & (lane_in - member * extra == lane_to - m * extra)
        rest += dot(quad_in[m, 1], jnp.where(move, 1.0, 0.0).astype(BF16), NN)
    block_out[QUAD] = rest.astype(BF16)

    def block_copy(k):
        return pltpu.make_async_remote_copy(
            src_ref=block_out,
            dst_ref=block_all.at[:, mine],
            send_sem=s3.at[k],
            recv_sem=r3.at[k],
            device_id={"head": head_peer(k)},
            device_id_type=MESH,
        )

    @pl.loop(0, HEAD_RANKS - 1)
    def _(i):
        block_copy(far_first(i, HEAD_RANKS)).start()

    block_all[:, mine, :] = block_out[...]
    q_row = rows_ref[...]
    lane = lax.broadcasted_iota(jnp.int32, (Y_SIZE * SLOT, 128), 1)
    pick = jnp.where(lane == q_row, 1.0, 0.0).astype(BF16)
    q_rest = jnp.where(q_row >= 128, q_row - 128, -1000)
    pick_rest = [
        jnp.where(lane == q_rest + m * extra, 1.0, 0.0).astype(BF16) for m in range(QUAD)
    ]

    @pl.loop(1, HEAD_RANKS)
    def _(k):
        block_copy(k).wait()

    cols = out_ref.shape[1]
    grad = jnp.zeros((Y_SIZE * SLOT, cols), F32)
    for m in range(QUAD):
        picked = dot(pick, block_all[m], NT) + dot(pick_rest[m], block_all[QUAD], NT)
        grad += dot(
            picked.astype(BF16), hidden_ref[m * cols : (m + 1) * cols, :], NT
        )
    full = cols // 128
    rest_rows = rows_out // 2
    y_out[...] = jnp.zeros_like(y_out)
    for y in range(Y_SIZE):
        piece = grad[y * SLOT : y * SLOT + rows_out]
        for t in range(full):
            y_out[y, t * rows_out : (t + 1) * rows_out, :] = piece[:, t * 128 : (t + 1) * 128]
        edge = piece[:, full * 128 :]
        y_out[y, full * rows_out : full * rows_out + rest_rows, :] = jnp.concatenate(
            (edge[:rest_rows], edge[rest_rows:]), axis=1
        )

    def y_copy(k):
        return pltpu.make_async_remote_copy(
            src_ref=y_out.at[y_peer(k)],
            dst_ref=y_in.at[k],
            send_sem=s4.at[k],
            recv_sem=r4.at[k],
            device_id={"dp": y_device(k)},
            device_id_type=MESH,
        )

    @pl.loop(0, Y_SIZE - 1)
    def _(i):
        y_copy(far_first(i, Y_SIZE)).start()

    first = y_out[y_pos]

    @pl.loop(1, Y_SIZE)
    def _(k):
        y_copy(k).wait()

    for k in range(1, Y_SIZE):
        first += y_in[k]
    for t in range(full):
        out_ref[:, t * 128 : (t + 1) * 128] = first[t * rows_out : (t + 1) * rows_out]
    edge = first[full * rows_out : full * rows_out + rest_rows]
    out_ref[:rest_rows, full * 128 :] = edge[:, :64]
    out_ref[rest_rows:, full * 128 :] = edge[:, 64:]


def fused_kernel(scale_factor, width, count, *refs):
    refs = list(refs)

    def take(n):
        taken = refs[:n]
        del refs[:n]
        return taken

    key_in, value_in, hidden_in, latent_ref, raw_ref, gain_ref = take(6)
    cos_t, sin_t, cos_ref, sin_ref, order_ref, rows_ref = take(6)
    loads = take(3)
    grad_query_ref, grad_rope_ref, out_ref = take(3)
    key_full, value_full, hidden_quad = take(3)
    latent, key_rot, total, rope_total, rope_part = take(5)
    buffers = take(3)
    load_sem = take(1)[0]
    gather_sems = take(9)

    copies = [
        pltpu.make_async_copy(loads[n], buffers[n], load_sem.at[n]) for n in range(3)
    ]

    def attention(enter):
        for copy in copies:
            copy.start()
        attention_start(
            latent_ref, raw_ref, gain_ref, cos_t, sin_t, latent, key_rot, total, rope_total
        )
        enter()
        finish = gather_body(
            key_in, value_in, hidden_in, key_full, value_full, hidden_quad, *gather_sems
        )
        for copy in copies:
            copy.wait()

        for pair in range(count):
            attention_pair(
                scale_factor, width, pair, *buffers, key_full, value_full,
                grad_query_ref, grad_rope_ref, latent, key_rot, total, rope_total,
            )

        finish()
        tokens, rope_width = rope_total.shape
        pairs = rope_total[...].reshape(tokens // CHUNK, 2, CHUNK // 2, rope_width)
        rope_part[...] = jnp.concatenate((pairs[:, 0], pairs[:, 1]), axis=2).reshape(
            tokens // 2, 2 * rope_width
        )

    tail_body(
        attention, total, rope_part, latent_ref, gain_ref, cos_ref, sin_ref, hidden_quad,
        order_ref, rows_ref, out_ref, *refs,
    )


def fused(
    key_up, value_up, hidden, latent_in, raw_key, gain, query, rope, cot, rows_out, dp_size
):
    tokens, rank = latent_in.shape
    cols = hidden.shape[0]
    rope_width = raw_key.shape[0]
    heads = rope.shape[1] // rope_width
    width = query.shape[1] // heads
    scale_factor = 1.0 / math.sqrt(width + rope_width)
    cos, sin = angle_tables(rope_width)
    order, rows = tail_tables(rows_out)
    dma = pltpu.SemaphoreType.DMA
    full = (key_up.shape[0] * dp_size, key_up.shape[1])
    any_spec = pl.BlockSpec(memory_space=pl.ANY)
    return pl.pallas_call(
        functools.partial(fused_kernel, scale_factor, width, heads // 2),
        out_shape=(
            jax.ShapeDtypeStruct(query.shape, BF16),
            jax.ShapeDtypeStruct(rope.shape, BF16),
            jax.ShapeDtypeStruct((rows_out, cols), F32),
        ),
        in_specs=[VMEM_SPEC] * 12 + [any_spec] * 3,
        out_specs=(VMEM_SPEC,) * 3,
        scratch_shapes=[
            pltpu.VMEM(full, BF16),
            pltpu.VMEM(full, BF16),
            pltpu.VMEM((QUAD * cols, tokens), BF16),
            pltpu.VMEM((tokens, rank), BF16),
            pltpu.VMEM((tokens, rope_width), BF16),
            pltpu.VMEM((tokens, rank), F32),
            pltpu.VMEM((tokens, rope_width), F32),
            pltpu.VMEM((tokens // 2, 2 * rope_width), F32),
            pltpu.VMEM(query.shape, BF16),
            pltpu.VMEM(rope.shape, BF16),
            pltpu.VMEM(cot.shape, BF16),
            dma((3,)),
            dma((21,)), dma((21,)), dma((9,)), dma((9,)), dma((32,)), dma((32,)), dma((3,)),
            dma((3,)), dma((3,)),
            pltpu.VMEM((HEAD_RANKS, CHUNK, rank), F32),
            pltpu.VMEM((HEAD_RANKS, CHUNK // 2, 128), F32),
            pltpu.VMEM((CHUNK, LANES), BF16),
            pltpu.VMEM((QUAD, 2, CHUNK, 128), BF16),
            pltpu.VMEM((QUAD, 2, CHUNK, 128), BF16),
            pltpu.VMEM((QUAD + 1, CHUNK, 128), BF16),
            pltpu.VMEM((QUAD + 1, tokens, 128), BF16),
            pltpu.VMEM((Y_SIZE, PACKED, 128), F32),
            pltpu.VMEM((Y_SIZE, PACKED, 128), F32),
            dma((HEAD_RANKS,)), dma((HEAD_RANKS,)), dma((QUAD,)), dma((QUAD,)),
            dma((HEAD_RANKS,)), dma((HEAD_RANKS,)), dma((Y_SIZE,)), dma((Y_SIZE,)),
            dma((HEAD_RANKS,)), dma((HEAD_RANKS,)),
        ],
        compiler_params=pltpu.CompilerParams(collective_id=1, has_side_effects=True),
        name="fused",
    )(
        key_up, value_up, hidden, latent_in, raw_key, gain,
        jnp.asarray(cos.T), jnp.asarray(sin.T), jnp.asarray(cos), jnp.asarray(sin),
        jnp.asarray(order), jnp.asarray(rows), query, rope, cot,
    )


def finish_kernel(
    token_total, query_in, rope_in, sum_ref, weight_ref, first_ref, second_ref,
    query_out, rope_out, new_weight_ref, new_first_ref, new_second_ref,
    query_buffer, rope_buffer, sems,
):
    chain = ((query_in, query_buffer, query_out), (rope_in, rope_buffer, rope_out))
    loads = [
        pltpu.make_async_copy(source, buffer, sems.at[n])
        for n, (source, buffer, _) in enumerate(chain)
    ]
    stores = [
        pltpu.make_async_copy(buffer, target, sems.at[2 + n])
        for n, (_, buffer, target) in enumerate(chain)
    ]
    for copy in loads:
        copy.start()
    for n in range(2):
        loads[n].wait()
        stores[n].start()
    weight_grad = sum_ref[...] / token_total
    new_first = beta_one * first_ref[...] + (1.0 - beta_one) * weight_grad
    new_second = beta_two * second_ref[...] + (1.0 - beta_two) * weight_grad * weight_grad
    direction = new_first / bias_one / (jnp.sqrt(new_second / bias_two) + adam_eps)
    weight = weight_ref[...]
    new_weight_ref[...] = weight - learn_rate * (direction + decay_rate * weight)
    new_first_ref[...] = new_first
    new_second_ref[...] = new_second
    for copy in stores:
        copy.wait()


def finish_step(token_total, grad_query, grad_rope, weight_sum, weight, first, second):
    any_spec = pl.BlockSpec(memory_space=pl.ANY)
    small = jax.ShapeDtypeStruct(weight.shape, F32)
    return pl.pallas_call(
        functools.partial(finish_kernel, float(token_total)),
        out_shape=(
            jax.ShapeDtypeStruct(grad_query.shape, BF16),
            jax.ShapeDtypeStruct(grad_rope.shape, BF16),
            small, small, small,
        ),
        in_specs=[any_spec] * 2 + [VMEM_SPEC] * 4,
        out_specs=(any_spec, any_spec, VMEM_SPEC, VMEM_SPEC, VMEM_SPEC),
        scratch_shapes=[
            pltpu.VMEM(grad_query.shape, BF16),
            pltpu.VMEM(grad_rope.shape, BF16),
            pltpu.SemaphoreType.DMA((4,)),
        ],
        name="finish_step",
    )(grad_query, grad_rope, weight_sum, weight, first, second)


def local(
    hidden_in,
    latent_unnormed,
    unrotated_key,
    latent_norm_scale,
    plain_query_rows,
    rotated_query_rows,
    key_up_matrix,
    value_up_matrix,
    output_cotangent,
    down_weight,
    first_moment,
    second_moment,
):
    row_count = latent_unnormed.shape[0]
    dp_size = lax.axis_size("dp")
    gain = latent_norm_scale[None, :]
    grad_query, grad_rope, weight_sum = fused(
        key_up_matrix, value_up_matrix, hidden_in.T, latent_unnormed, unrotated_key.T, gain,
        plain_query_rows, rotated_query_rows, output_cotangent, down_weight.shape[0], dp_size,
    )
    return finish_step(
        row_count * dp_size, grad_query, grad_rope, weight_sum,
        down_weight, first_moment, second_moment,
    )


def solution(mesh):
    placed = (
        P("dp", "head"),
        P("dp", None),
        P("dp", None),
        P(),
        P("dp", "head"),
        P("dp", "head"),
        P("dp", "head"),
        P("dp", "head"),
        P("dp", "head"),
        P("dp", "head"),
        P("dp", "head"),
        P("dp", "head"),
    )
    return jax.shard_map(
        local,
        mesh=mesh,
        in_specs=placed,
        out_specs=(
            P("dp", "head"),
            P("dp", "head"),
            P("dp", "head"),
            P("dp", "head"),
            P("dp", "head"),
        ),
        check_vma=False,
    )
```

```python
import functools
import math

import jax
import jax.numpy as jnp
import numpy as np
from jax import lax
from jax.experimental import pallas as pl
from jax.experimental.pallas import tpu as pltpu
from jax.sharding import PartitionSpec as P

SEQUENCE_LENGTH = 256

norm_eps = 1e-06
beta_one = 0.9
beta_two = 0.999
adam_eps = 1e-08
learn_rate = 0.01
decay_rate = 0.1
bias_one = 1.0 - 0.9**2
bias_two = 1.0 - 0.999**2

MESH = pl.DeviceIdType.MESH
BF16 = jnp.bfloat16
F32 = jnp.float32

Y_SIZE = 8
HEAD_RANKS = 16
LANES = 640
CHUNK = 16
SLOT = 24
PACKED = 64
QUAD = 4
VMEM_SPEC = pl.BlockSpec(memory_space=pltpu.VMEM)


def angle_tables(rope_width):
    half_width = rope_width // 2
    inverse_freq = np.exp(
        np.arange(half_width, dtype=np.float32)
        * np.float32(-2.0 * math.log(10000.0) / rope_width)
    ).astype(np.float32)
    angles = np.arange(SEQUENCE_LENGTH, dtype=np.float32)[:, None] * inverse_freq[None, :]
    return np.cos(angles).astype(np.float32), np.sin(angles).astype(np.float32)


def gather_body(
    key_ref, value_ref, hidden_ref, key_out, value_out, hidden_out,
    y_send, y_recv, x_send, x_recv, c_send, c_recv, own_sem, h_send, h_recv,
):
    dp = lax.axis_index("dp")
    core = lax.rem(dp, 2)
    chip = dp // 2
    y_pos = lax.rem(chip, Y_SIZE)
    x_pos = chip // Y_SIZE

    def place(x, y, c):
        return (x * Y_SIZE + lax.rem(y + Y_SIZE, Y_SIZE)) * 2 + c

    other_x = 1 - x_pos
    ups = (place(x_pos, y_pos + 1, core), place(x_pos, y_pos - 1, core))
    x_partner = place(other_x, y_pos, core)
    c_partner = place(x_pos, y_pos, 1 - core)

    rows_in = key_ref.shape[0]
    sources = (key_ref, value_ref)
    outs = (key_out, value_out)

    def rows_of(index):
        return pl.ds(pl.multiple_of(index * rows_in, rows_in), rows_in)

    def send(w, src, block, sems, e, peer):
        copy = pltpu.make_async_remote_copy(
            src_ref=src,
            dst_ref=outs[w].at[rows_of(block)],
            send_sem=sems[0].at[e],
            recv_sem=sems[1].at[e],
            device_id={"dp": peer},
            device_id_type=MESH,
        )
        copy.start()
        return copy

    y_sems, x_sems, c_sems = (y_send, y_recv), (x_send, x_recv), (c_send, c_recv)
    steps = {(0, 0): 4, (0, 1): 3, (1, 0): 3, (1, 1): 4}
    event = {}
    for s in range(1, 5):
        for p, w in ((0, 0), (0, 1), (1, 0)):
            for d in range(2):
                if s <= steps[(w, d)]:
                    event[(s, p, w, d)] = len(event)
    late = {}
    for s in range(1, 5):
        for d in range(2):
            if s <= steps[(1, d)]:
                late[(s, d)] = len(late)
    y_copies, x_copies, c_copies = {}, {}, {}

    for w in range(2):
        x_copies[w] = send(w, sources[w], dp, x_sems, w, x_partner)
    for w in range(2):
        for d in range(2):
            e = event[(1, 0, w, d)]
            y_copies[e] = send(w, sources[w], dp, y_sems, e, ups[d])
    for w in range(2):
        c_copies[w] = send(w, sources[w], dp, c_sems, w, c_partner)
    own = []
    for w in range(2):
        copy = pltpu.make_async_copy(sources[w], outs[w].at[rows_of(dp)], own_sem.at[w])
        copy.start()
        own.append(copy)
    def hidden_rows(x, c):
        size = hidden_ref.shape[0]
        return hidden_out.at[pl.ds(pl.multiple_of((x * 2 + c) * size, size), size)]

    def send_hidden(src, dst, e, peer):
        copy = pltpu.make_async_remote_copy(
            src_ref=src,
            dst_ref=dst,
            send_sem=h_send.at[e],
            recv_sem=h_recv.at[e],
            device_id={"dp": peer},
            device_id_type=MESH,
        )
        copy.start()
        return copy

    hidden_x = send_hidden(hidden_ref, hidden_rows(x_pos, core), 0, x_partner)
    hidden_c = send_hidden(hidden_ref, hidden_rows(x_pos, core), 1, c_partner)
    copy = pltpu.make_async_copy(hidden_ref, hidden_rows(x_pos, core), own_sem.at[2])
    copy.start()
    own.append(copy)
    for w in range(2):
        x_copies[w].wait_recv()
        view = outs[w].at[rows_of(x_partner)]
        if w == 0:
            for d in range(2):
                e = event[(1, 1, w, d)]
                y_copies[e] = send(w, view, x_partner, y_sems, e, ups[d])
        c_copies[2 + w] = send(w, view, x_partner, c_sems, 2 + w, c_partner)

    def near(s, d):
        return y_pos - s if d == 0 else y_pos + s

    def take_late(s):
        for d in range(2):
            if (s, d) in late:
                e = late[(s, d)]
                block = place(other_x, near(s, d), core)
                x_copies[2 + e].wait_recv()
                view = outs[1].at[rows_of(block)]
                n = 4 + len(event) + e
                c_copies[n] = send(1, view, block, c_sems, n, c_partner)

    for s in range(1, 5):
        for (step, p, w, d), e in event.items():
            if step != s:
                continue
            block = place(x_pos if p == 0 else other_x, near(s, d), core)
            y_copies[e].wait_recv()
            view = outs[w].at[rows_of(block)]
            if s < steps[(w, d)]:
                n = event[(s + 1, p, w, d)]
                y_copies[n] = send(w, view, block, y_sems, n, ups[d])
            if w == 1:
                n = 2 + late[(s, d)]
                x_copies[n] = send(w, view, block, x_sems, n, x_partner)
            c_copies[4 + e] = send(w, view, block, c_sems, 4 + e, c_partner)
        if s > 1:
            take_late(s - 1)
    take_late(4)
    hidden_x.wait_recv()
    far = hidden_rows(other_x, core)
    hidden_d = send_hidden(far, far, 2, c_partner)
    for copy in own:
        copy.wait()
    for copy in c_copies.values():
        copy.wait_recv()

    def finish():
        for group in (x_copies, y_copies, c_copies):
            for copy in group.values():
                copy.wait_send()
        hidden_x.wait_send()
        hidden_c.wait()
        hidden_d.wait()

    return finish


def dot(a, b, dims):
    return lax.dot_general(a, b, (dims, ((), ())), preferred_element_type=F32)


NN = ((1,), (0,))
NT = ((1,), (1,))
TN = ((0,), (0,))


def attention_start(latent_ref, raw_ref, gain_ref, cos_ref, sin_ref, latent, key_rot, total, rope_total):
    half = raw_ref.shape[0] // 2
    x = latent_ref[...].astype(F32)
    inv = lax.rsqrt(jnp.mean(x * x, axis=1, keepdims=True) + norm_eps)
    latent[...] = (x * inv * gain_ref[...]).astype(BF16)
    raw = raw_ref[...].astype(F32)
    u, w = raw[:half], raw[half:]
    cos, sin = cos_ref[...], sin_ref[...]
    rotated = jnp.concatenate((u * cos - w * sin, u * sin + w * cos), axis=0)
    key_rot[...] = rotated.T.astype(BF16)
    total[...] = jnp.zeros_like(total)
    rope_total[...] = jnp.zeros_like(rope_total)


def attention_pair(
    scale_factor, width, pair,
    query_ref, rope_ref, cot_ref, key_up_ref, value_up_ref, grad_query_ref, grad_rope_ref,
    latent, key_rot, total, rope_total,
):
    tokens = latent.shape[0]
    rope_width = key_rot.shape[1]

    def columns(size):
        return slice(pair * size, (pair + 1) * size)

    both = columns(2 * width)
    key_up, value_up = key_up_ref[:, both], value_up_ref[:, both]
    queries, cots = query_ref[:, both], cot_ref[:, both]
    ropes = rope_ref[:, columns(2 * rope_width)]
    keys2 = dot(latent[...], key_up, NN).astype(BF16)
    values2 = dot(latent[...], value_up, NN).astype(BF16)
    rot = key_rot[...]
    causal = lax.broadcasted_iota(jnp.int32, (tokens, tokens), 0) <= lax.broadcasted_iota(
        jnp.int32, (tokens, tokens), 1
    )
    grad_queries, grad_keys, grad_values, grad_ropes = [], [], [], []
    for h in range(2):
        cols = slice(h * width, (h + 1) * width)
        query = queries[:, cols]
        rope = ropes[:, h * rope_width : (h + 1) * rope_width]
        cot = cots[:, cols]
        key = keys2[:, cols]
        value = values2[:, cols]
        scores = (dot(key, query, NT) + dot(rot, rope, NT)) * scale_factor
        scores = jnp.where(causal, scores, -1e30)
        grown = jnp.exp(scores - jnp.max(scores, axis=0, keepdims=True))
        probs = grown * (1.0 / jnp.sum(grown, axis=0, keepdims=True))
        prob_low = probs.astype(BF16)
        grad_probs = dot(value, cot, NT)
        delta = jnp.sum(prob_low.astype(F32) * grad_probs, axis=0, keepdims=True)
        score_low = (probs * (grad_probs - delta) * scale_factor).astype(BF16)
        grad_queries.append(dot(score_low, key, TN).astype(BF16))
        grad_ropes.append(dot(score_low, rot, TN).astype(BF16))
        grad_keys.append(dot(score_low, query, NN).astype(BF16))
        grad_values.append(dot(prob_low, cot, NN).astype(BF16))
        rope_total[...] += dot(score_low, rope, NN)
    grad_query_ref[:, both] = jnp.concatenate(grad_queries, axis=1)
    grad_rope_ref[:, columns(2 * rope_width)] = jnp.concatenate(grad_ropes, axis=1)
    total[...] += dot(jnp.concatenate(grad_keys, axis=1), key_up, NT) + dot(
        jnp.concatenate(grad_values, axis=1), value_up, NT
    )


def tail_tables(rows_out):
    per_quad = Y_SIZE * rows_out

    def column(member, q):
        y, r = divmod(q, rows_out)
        return (((member // 2) * Y_SIZE + y) * 2 + member % 2) * rows_out + r

    extra = per_quad - 128
    order = np.full((1, (QUAD + 1) * 128), -1, np.int32)
    for member in range(QUAD):
        for q in range(per_quad):
            lane = member * 128 + q if q < 128 else QUAD * 128 + member * extra + q - 128
            order[0, lane] = column(member, q)
    rows = np.full((Y_SIZE * SLOT, 1), -1000, np.int32)
    for y in range(Y_SIZE):
        rows[y * SLOT : y * SLOT + rows_out, 0] = y * rows_out + np.arange(rows_out)
    return order, rows


def far_first(i, size):
    return size // 2 + (1 - 2 * lax.rem(i, 2)) * ((i + 1) // 2)


def tail_body(
    attention, part_ref, rope_part_ref, latent_ref, gain_ref, cos_ref, sin_ref, hidden_ref, order_ref,
    rows_ref, out_ref, sum_recv, rope_recv, kv_own, quad_out, quad_in, block_out, block_all, y_out, y_in,
    s1, r1, s2, r2, s3, r3, s4, r4, s5, r5,
):
    dp = lax.axis_index("dp")
    head = lax.axis_index("head")
    core = lax.rem(dp, 2)
    chip = dp // 2
    y_pos = lax.rem(chip, Y_SIZE)
    x_pos = chip // Y_SIZE
    member = x_pos * 2 + core
    rank = latent_ref.shape[1]
    tokens = latent_ref.shape[0]
    rope_width = 2 * cos_ref.shape[1]
    half = rope_width // 2
    rows_out = out_ref.shape[0]
    kv_width = rank + rope_width
    extra = Y_SIZE * rows_out - 128

    def head_peer(k):
        return lax.rem(head + k, HEAD_RANKS)

    def y_peer(k):
        return lax.rem(y_pos + k, Y_SIZE)

    def y_device(k):
        return (x_pos * Y_SIZE + y_peer(k)) * 2 + core

    def quad_peer(k):
        return lax.rem(member + k, QUAD)

    def quad_device(k):
        other = quad_peer(k)
        return ((other // 2) * Y_SIZE + y_pos) * 2 + lax.rem(other, 2)

    barrier = pltpu.get_barrier_semaphore()

    @pl.loop(1, HEAD_RANKS)
    def _(k):
        pl.semaphore_signal(barrier, inc=1, device_id={"head": head_peer(k)}, device_id_type=MESH)

    @pl.loop(1, Y_SIZE)
    def _(k):
        pl.semaphore_signal(barrier, inc=1, device_id={"dp": y_device(k)}, device_id_type=MESH)

    @pl.loop(1, QUAD)
    def _(k):
        pl.semaphore_signal(barrier, inc=1, device_id={"dp": quad_device(k)}, device_id_type=MESH)

    attention(lambda: pl.semaphore_wait(barrier, HEAD_RANKS - 1 + Y_SIZE - 1 + QUAD - 1))

    def rows_of(index, size):
        return pl.ds(pl.multiple_of(index * size, size), size)

    def sum_copy(k):
        return pltpu.make_async_remote_copy(
            src_ref=part_ref.at[rows_of(head_peer(k), CHUNK)],
            dst_ref=sum_recv.at[k],
            send_sem=s1.at[k],
            recv_sem=r1.at[k],
            device_id={"head": head_peer(k)},
            device_id_type=MESH,
        )

    def rope_copy(k):
        return pltpu.make_async_remote_copy(
            src_ref=rope_part_ref.at[rows_of(head_peer(k), CHUNK // 2)],
            dst_ref=rope_recv.at[k],
            send_sem=s5.at[k],
            recv_sem=r5.at[k],
            device_id={"head": head_peer(k)},
            device_id_type=MESH,
        )

    @pl.loop(0, HEAD_RANKS - 1)
    def _(i):
        k = far_first(i, HEAD_RANKS)
        sum_copy(k).start()
        rope_copy(k).start()

    mine = rows_of(head, CHUNK)
    x = latent_ref[mine, :].astype(F32)
    inv = lax.rsqrt(jnp.mean(x * x, axis=1, keepdims=True) + norm_eps)
    cos, sin = cos_ref[mine, :], sin_ref[mine, :]
    total = part_ref[mine, :]
    rope_sum = rope_part_ref[rows_of(head, CHUNK // 2), :]
    iota = lax.broadcasted_iota(jnp.int32, (LANES, LANES), 0)
    select = jnp.where(iota == order_ref[...], 1.0, 0.0).astype(BF16)

    @pl.loop(1, HEAD_RANKS)
    def _(k):
        sum_copy(k).wait()
        rope_copy(k).wait()

    for k in range(1, HEAD_RANKS):
        total += sum_recv[k]
        rope_sum += rope_recv[k]
    scaled = gain_ref[...] * total
    inner = jnp.sum(x * scaled, axis=1, keepdims=True)
    latent_grad = inv * scaled - x * (inv * inv * inv) * inner / rank
    rope_sum = jnp.concatenate((rope_sum[:, :rope_width], rope_sum[:, rope_width:]), axis=0)
    g, q = rope_sum[:, :half], rope_sum[:, half:]
    rope_grad = jnp.concatenate(
        (
            g * cos + q * sin,
            q * cos - g * sin,
            jnp.zeros((CHUNK, LANES - kv_width), F32),
        ),
        axis=1,
    )
    kv_own[:, :rank] = latent_grad.astype(BF16)
    kv_own[:, rank:] = rope_grad.astype(BF16)

    sent = dot(kv_own[...], select, NN).astype(BF16)
    for m in range(QUAD):
        quad_out[m, 0] = sent[:, m * 128 : (m + 1) * 128]
        quad_out[m, 1] = sent[:, QUAD * 128 :]

    def quad_copy(k):
        return pltpu.make_async_remote_copy(
            src_ref=quad_out.at[quad_peer(k)],
            dst_ref=quad_in.at[member],
            send_sem=s2.at[k],
            recv_sem=r2.at[k],
            device_id={"dp": quad_device(k)},
            device_id_type=MESH,
        )

    for k in range(1, QUAD):
        quad_copy(k).start()
    quad_in[member] = quad_out[member]
    lane_in = lax.broadcasted_iota(jnp.int32, (128, 128), 0)
    lane_to = lax.broadcasted_iota(jnp.int32, (128, 128), 1)
    for k in range(1, QUAD):
        quad_copy(k).wait()
    rest = jnp.zeros((CHUNK, 128), F32)
    for m in range(QUAD):
        block_out[m] = quad_in[m, 0]
        inside = (lane_to >= m * extra) & (lane_to < (m + 1) * extra)
        move = inside & (lane_in - member * extra == lane_to - m * extra)
        rest += dot(quad_in[m, 1], jnp.where(move, 1.0, 0.0).astype(BF16), NN)
    block_out[QUAD] = rest.astype(BF16)

    def block_copy(k):
        return pltpu.make_async_remote_copy(
            src_ref=block_out,
            dst_ref=block_all.at[:, mine],
            send_sem=s3.at[k],
            recv_sem=r3.at[k],
            device_id={"head": head_peer(k)},
            device_id_type=MESH,
        )

    @pl.loop(0, HEAD_RANKS - 1)
    def _(i):
        block_copy(far_first(i, HEAD_RANKS)).start()

    block_all[:, mine, :] = block_out[...]
    q_row = rows_ref[...]
    lane = lax.broadcasted_iota(jnp.int32, (Y_SIZE * SLOT, 128), 1)
    pick = jnp.where(lane == q_row, 1.0, 0.0).astype(BF16)
    q_rest = jnp.where(q_row >= 128, q_row - 128, -1000)
    pick_rest = [
        jnp.where(lane == q_rest + m * extra, 1.0, 0.0).astype(BF16) for m in range(QUAD)
    ]

    @pl.loop(1, HEAD_RANKS)
    def _(k):
        block_copy(k).wait()

    cols = out_ref.shape[1]
    grad = jnp.zeros((Y_SIZE * SLOT, cols), F32)
    for m in range(QUAD):
        picked = dot(pick, block_all[m], NT) + dot(pick_rest[m], block_all[QUAD], NT)
        grad += dot(
            picked.astype(BF16), hidden_ref[m * cols : (m + 1) * cols, :], NT
        )
    full = cols // 128
    rest_rows = rows_out // 2
    y_out[...] = jnp.zeros_like(y_out)
    for y in range(Y_SIZE):
        piece = grad[y * SLOT : y * SLOT + rows_out]
        for t in range(full):
            y_out[y, t * rows_out : (t + 1) * rows_out, :] = piece[:, t * 128 : (t + 1) * 128]
        edge = piece[:, full * 128 :]
        y_out[y, full * rows_out : full * rows_out + rest_rows, :] = jnp.concatenate(
            (edge[:rest_rows], edge[rest_rows:]), axis=1
        )

    def y_copy(k):
        return pltpu.make_async_remote_copy(
            src_ref=y_out.at[y_peer(k)],
            dst_ref=y_in.at[k],
            send_sem=s4.at[k],
            recv_sem=r4.at[k],
            device_id={"dp": y_device(k)},
            device_id_type=MESH,
        )

    @pl.loop(0, Y_SIZE - 1)
    def _(i):
        y_copy(far_first(i, Y_SIZE)).start()

    first = y_out[y_pos]

    @pl.loop(1, Y_SIZE)
    def _(k):
        y_copy(k).wait()

    for k in range(1, Y_SIZE):
        first += y_in[k]
    for t in range(full):
        out_ref[:, t * 128 : (t + 1) * 128] = first[t * rows_out : (t + 1) * rows_out]
    edge = first[full * rows_out : full * rows_out + rest_rows]
    out_ref[:rest_rows, full * 128 :] = edge[:, :64]
    out_ref[rest_rows:, full * 128 :] = edge[:, 64:]


def fused_kernel(scale_factor, width, count, *refs):
    refs = list(refs)

    def take(n):
        taken = refs[:n]
        del refs[:n]
        return taken

    key_in, value_in, hidden_in, latent_ref, raw_ref, gain_ref = take(6)
    cos_t, sin_t, cos_ref, sin_ref, order_ref, rows_ref = take(6)
    loads = take(3)
    query_out, rope_out, out_ref = take(3)
    key_full, value_full, hidden_quad = take(3)
    latent, key_rot, total, rope_total, rope_part = take(5)
    buffers = take(3)
    grad_query_ref, grad_rope_ref = take(2)
    load_sem = take(1)[0]
    gather_sems = take(9)

    copies = [
        pltpu.make_async_copy(loads[n], buffers[n], load_sem.at[n]) for n in range(3)
    ]

    stores = [
        pltpu.make_async_copy(grad_query_ref, query_out, load_sem.at[3]),
        pltpu.make_async_copy(grad_rope_ref, rope_out, load_sem.at[4]),
    ]

    def attention(enter):
        for copy in copies:
            copy.start()
        attention_start(
            latent_ref, raw_ref, gain_ref, cos_t, sin_t, latent, key_rot, total, rope_total
        )
        enter()
        finish = gather_body(
            key_in, value_in, hidden_in, key_full, value_full, hidden_quad, *gather_sems
        )
        for copy in copies:
            copy.wait()

        for pair in range(count):
            attention_pair(
                scale_factor, width, pair, *buffers, key_full, value_full,
                grad_query_ref, grad_rope_ref, latent, key_rot, total, rope_total,
            )

        for copy in stores:
            copy.start()
        finish()
        tokens, rope_width = rope_total.shape
        pairs = rope_total[...].reshape(tokens // CHUNK, 2, CHUNK // 2, rope_width)
        rope_part[...] = jnp.concatenate((pairs[:, 0], pairs[:, 1]), axis=2).reshape(
            tokens // 2, 2 * rope_width
        )

    tail_body(
        attention, total, rope_part, latent_ref, gain_ref, cos_ref, sin_ref, hidden_quad,
        order_ref, rows_ref, out_ref, *refs,
    )
    for copy in stores:
        copy.wait()


def fused(
    key_up, value_up, hidden, latent_in, raw_key, gain, query, rope, cot, rows_out, dp_size
):
    tokens, rank = latent_in.shape
    cols = hidden.shape[0]
    rope_width = raw_key.shape[0]
    heads = rope.shape[1] // rope_width
    width = query.shape[1] // heads
    scale_factor = 1.0 / math.sqrt(width + rope_width)
    cos, sin = angle_tables(rope_width)
    order, rows = tail_tables(rows_out)
    dma = pltpu.SemaphoreType.DMA
    full = (key_up.shape[0] * dp_size, key_up.shape[1])
    any_spec = pl.BlockSpec(memory_space=pl.ANY)
    return pl.pallas_call(
        functools.partial(fused_kernel, scale_factor, width, heads // 2),
        out_shape=(
            jax.ShapeDtypeStruct(query.shape, BF16),
            jax.ShapeDtypeStruct(rope.shape, BF16),
            jax.ShapeDtypeStruct((rows_out, cols), F32),
        ),
        in_specs=[VMEM_SPEC] * 12 + [any_spec] * 3,
        out_specs=(any_spec, any_spec, VMEM_SPEC),
        scratch_shapes=[
            pltpu.VMEM(full, BF16),
            pltpu.VMEM(full, BF16),
            pltpu.VMEM((QUAD * cols, tokens), BF16),
            pltpu.VMEM((tokens, rank), BF16),
            pltpu.VMEM((tokens, rope_width), BF16),
            pltpu.VMEM((tokens, rank), F32),
            pltpu.VMEM((tokens, rope_width), F32),
            pltpu.VMEM((tokens // 2, 2 * rope_width), F32),
            pltpu.VMEM(query.shape, BF16),
            pltpu.VMEM(rope.shape, BF16),
            pltpu.VMEM(cot.shape, BF16),
            pltpu.VMEM(query.shape, BF16),
            pltpu.VMEM(rope.shape, BF16),
            dma((5,)),
            dma((21,)), dma((21,)), dma((9,)), dma((9,)), dma((32,)), dma((32,)), dma((3,)),
            dma((3,)), dma((3,)),
            pltpu.VMEM((HEAD_RANKS, CHUNK, rank), F32),
            pltpu.VMEM((HEAD_RANKS, CHUNK // 2, 128), F32),
            pltpu.VMEM((CHUNK, LANES), BF16),
            pltpu.VMEM((QUAD, 2, CHUNK, 128), BF16),
            pltpu.VMEM((QUAD, 2, CHUNK, 128), BF16),
            pltpu.VMEM((QUAD + 1, CHUNK, 128), BF16),
            pltpu.VMEM((QUAD + 1, tokens, 128), BF16),
            pltpu.VMEM((Y_SIZE, PACKED, 128), F32),
            pltpu.VMEM((Y_SIZE, PACKED, 128), F32),
            dma((HEAD_RANKS,)), dma((HEAD_RANKS,)), dma((QUAD,)), dma((QUAD,)),
            dma((HEAD_RANKS,)), dma((HEAD_RANKS,)), dma((Y_SIZE,)), dma((Y_SIZE,)),
            dma((HEAD_RANKS,)), dma((HEAD_RANKS,)),
        ],
        compiler_params=pltpu.CompilerParams(collective_id=1, has_side_effects=True),
        name="fused",
    )(
        key_up, value_up, hidden, latent_in, raw_key, gain,
        jnp.asarray(cos.T), jnp.asarray(sin.T), jnp.asarray(cos), jnp.asarray(sin),
        jnp.asarray(order), jnp.asarray(rows), query, rope, cot,
    )


def finish_kernel(
    token_total, query_in, rope_in, sum_ref, weight_ref, first_ref, second_ref,
    query_out, rope_out, new_weight_ref, new_first_ref, new_second_ref,
    query_buffer, rope_buffer, sems,
):
    chain = ((query_in, query_buffer, query_out), (rope_in, rope_buffer, rope_out))
    loads = [
        pltpu.make_async_copy(source, buffer, sems.at[n])
        for n, (source, buffer, _) in enumerate(chain)
    ]
    stores = [
        pltpu.make_async_copy(buffer, target, sems.at[2 + n])
        for n, (_, buffer, target) in enumerate(chain)
    ]
    for copy in loads:
        copy.start()
    for n in range(2):
        loads[n].wait()
        stores[n].start()
    weight_grad = sum_ref[...] / token_total
    new_first = beta_one * first_ref[...] + (1.0 - beta_one) * weight_grad
    new_second = beta_two * second_ref[...] + (1.0 - beta_two) * weight_grad * weight_grad
    direction = new_first / bias_one / (jnp.sqrt(new_second / bias_two) + adam_eps)
    weight = weight_ref[...]
    new_weight_ref[...] = weight - learn_rate * (direction + decay_rate * weight)
    new_first_ref[...] = new_first
    new_second_ref[...] = new_second
    for copy in stores:
        copy.wait()


def finish_step(token_total, grad_query, grad_rope, weight_sum, weight, first, second):
    any_spec = pl.BlockSpec(memory_space=pl.ANY)
    small = jax.ShapeDtypeStruct(weight.shape, F32)
    return pl.pallas_call(
        functools.partial(finish_kernel, float(token_total)),
        out_shape=(
            jax.ShapeDtypeStruct(grad_query.shape, BF16),
            jax.ShapeDtypeStruct(grad_rope.shape, BF16),
            small, small, small,
        ),
        in_specs=[any_spec] * 2 + [VMEM_SPEC] * 4,
        out_specs=(any_spec, any_spec, VMEM_SPEC, VMEM_SPEC, VMEM_SPEC),
        scratch_shapes=[
            pltpu.VMEM(grad_query.shape, BF16),
            pltpu.VMEM(grad_rope.shape, BF16),
            pltpu.SemaphoreType.DMA((4,)),
        ],
        name="finish_step",
    )(grad_query, grad_rope, weight_sum, weight, first, second)


def local(
    hidden_in,
    latent_unnormed,
    unrotated_key,
    latent_norm_scale,
    plain_query_rows,
    rotated_query_rows,
    key_up_matrix,
    value_up_matrix,
    output_cotangent,
    down_weight,
    first_moment,
    second_moment,
):
    row_count = latent_unnormed.shape[0]
    dp_size = lax.axis_size("dp")
    gain = latent_norm_scale[None, :]
    grad_query, grad_rope, weight_sum = fused(
        key_up_matrix, value_up_matrix, hidden_in.T, latent_unnormed, unrotated_key.T, gain,
        plain_query_rows, rotated_query_rows, output_cotangent, down_weight.shape[0], dp_size,
    )
    return finish_step(
        row_count * dp_size, grad_query, grad_rope, weight_sum,
        down_weight, first_moment, second_moment,
    )


def solution(mesh):
    placed = (
        P("dp", "head"),
        P("dp", None),
        P("dp", None),
        P(),
        P("dp", "head"),
        P("dp", "head"),
        P("dp", "head"),
        P("dp", "head"),
        P("dp", "head"),
        P("dp", "head"),
        P("dp", "head"),
        P("dp", "head"),
    )
    return jax.shard_map(
        local,
        mesh=mesh,
        in_specs=placed,
        out_specs=(
            P("dp", "head"),
            P("dp", "head"),
            P("dp", "head"),
            P("dp", "head"),
            P("dp", "head"),
        ),
        check_vma=False,
    )
```
